32 devices in a mesh: dp: 8 (over y, x, core), layer: 4 (over z).
Axes of the slice: x: 2, y: 2, z: 4, core: 2. Of those that a mesh axis runs over, the one named last changes fastest.
Arguments:
- output_gradient: bfloat16 [2, 4, 128, 8, 8192], P(None, 'layer', 'dp'), may hold values from -20 to 20, as said below
- adapter_activation: bfloat16 [2, 4, 128, 8, 128], P(None, 'layer', 'dp'), may hold values from -6 to 6
- adaptive_variance: bfloat16 [2, 4, 8192, 128], P(None, 'layer'), may hold values from 0.0099487305 to 1
- holdout_feature: bfloat16 [2, 4, 64, 5120], P(None, 'layer', 'dp'), may hold values from -6 to 6
- lengths: int32 [128], P('dp'), may hold values from 1 to 8
- token_loss_mask: int32 [128, 8], P('dp'), may hold values 0 or 1
- sketch_seed: int32 [1], replicated, may hold values from 0 to 1048575
- step_size_weight: float32 [2], replicated, may hold values from 0.5 to 2
Outputs:
- scores: float32 [128, 64], P(('dp', 'layer'))
The draws below stay inside these ranges and needn't reach their ends.
Inputs may be any that keep to these rules, and one draw needn't show every extreme that they name: Entries of output_gradient and adapter_activation at token slots where valid is 0 may hold any finite values within the stated range.
All inputs are finite; a program needn't handle non-finite values. No bound on the sum of `token_loss_mask` on one device may be relied on, other than what follows from the above.
Results may differ from the reference program's by a relative error of at most 0.004.
Values may be sent and summed in bfloat16 or wider, within the bound.
No kernel may reach another device: no remote copies, remote signals or barrier semaphores. Data moves between devices by JAX's collectives and lax.ppermute only.
A program may use at most 64 MiB of HBM per device.

```python
import math
import jax
import jax.numpy as jnp
from jax import lax

D = 8192
ADAPTER_RANK = 128
KL = 40
KF = 5120
SAVED_POINTS = 2
MODEL_LAYERS = 4
TOKEN_SLOTS = 8
TRAIN_SAMPLES = 128
NVAL = 64


def draw_output_gradient(key, part):
    full_shape = (SAVED_POINTS, MODEL_LAYERS, TRAIN_SAMPLES, TOKEN_SLOTS, D)
    layer_depth = jnp.arange(MODEL_LAYERS, dtype=jnp.float32) / max(MODEL_LAYERS - 1, 1)
    values = jnp.clip(jax.random.normal(key, full_shape, jnp.float32), -6.0, 6.0)
    layer_ramp = 0.6 * 2.0 ** layer_depth
    return (values * layer_ramp[None, :, None, None, None]).astype(jnp.bfloat16)


def plant(drawn, rng, low, top_value):
    place = [jax.random.randint(jax.random.fold_in(rng, axis), (), 0, length) for axis, length in enumerate(drawn.shape)]
    main_axis = drawn.shape.index(max(drawn.shape))
    next_to = place[:main_axis] + [(place[main_axis] + 1) % drawn.shape[main_axis]] + place[main_axis + 1:]
    return drawn.at[tuple(place)].set(low).at[tuple(next_to)].set(top_value)


def block_scale(own_key, dims, cuts, least, high):
    gain, own = 1.0, jax.random.fold_in(own_key, 6)
    for axis_at, shards_of in cuts:
        heights = jnp.exp(jax.random.uniform(jax.random.fold_in(own, axis_at), (shards_of,), jnp.float32, least / len(cuts), high / len(cuts)))
        gain = gain * jnp.repeat(heights, dims[axis_at] // shards_of).reshape([-1 if axis == axis_at else 1 for axis in range(len(dims))])
    return gain


def scatter_about(own_key, shape, scale, limit, pieces=(), kind=jnp.bfloat16):
    level = block_scale(own_key, shape, pieces, -0.22, 0.18) if pieces else 1.0
    result = jax.random.normal(own_key, shape, jnp.float32) * scale * level
    return jnp.minimum(jnp.maximum(result, -limit), limit).astype(kind)


def setup_inputs(seed: int = 0) -> dict:
    streams_of = jax.random.split(jax.random.key(seed), 9)
    output_gradient = draw_output_gradient(jax.random.fold_in(streams_of[8], 71), 0)
    adapter_activation = scatter_about(streams_of[1], (SAVED_POINTS, MODEL_LAYERS, TRAIN_SAMPLES, TOKEN_SLOTS, ADAPTER_RANK), 1.0, 6.0, ((1, 4), (2, 8)))
    adaptive_variance = jnp.clip(jnp.exp(math.log(1.0) - 4.61031033 * jax.random.uniform(streams_of[2], (SAVED_POINTS, MODEL_LAYERS, D, ADAPTER_RANK), jnp.float32) ** block_scale(streams_of[2], (SAVED_POINTS, MODEL_LAYERS, D, ADAPTER_RANK), ((1, 4),), -0.2, 0.2)), 0.0099487305, 1.0).astype(jnp.bfloat16)
    holdout_feature = scatter_about(streams_of[3], (SAVED_POINTS, MODEL_LAYERS, NVAL, KF), 1.0, 6.0, ((1, 4), (2, 8)))
    lengths = plant(jax.random.randint(streams_of[4], (TRAIN_SAMPLES,), 1, TOKEN_SLOTS + 1), jax.random.fold_in(streams_of[4], 1), 1, TOKEN_SLOTS).astype(jnp.int32)
    token_loss_mask = plant((jax.random.randint(streams_of[5], (TRAIN_SAMPLES, TOKEN_SLOTS), 0, 4) < 3).astype(jnp.int32), jax.random.fold_in(streams_of[5], 1), 0, 1)
    sketch_seed = jax.random.randint(streams_of[6], (1,), 0, 1048576).astype(jnp.int32)
    step_size_weight = jnp.clip(jax.random.uniform(streams_of[7], (SAVED_POINTS,), jnp.float32, 0.5, 2.0), 0.5, 2.0)
    return {"output_gradient": output_gradient, "adapter_activation": adapter_activation, "adaptive_variance": adaptive_variance, "holdout_feature": holdout_feature, "lengths": lengths, "token_loss_mask": token_loss_mask, "sketch_seed": sketch_seed, "step_size_weight": step_size_weight}


def projection(seed_value, layer_id, width, columns):
    row_ids = jnp.arange(width, dtype=jnp.int32)[:, None]
    col_ids = jnp.arange(columns, dtype=jnp.int32)[None, :]
    hashed = row_ids * 1103515245 + col_ids * 12345 + layer_id * 668265263 + seed_value * 374761393
    hashed = hashed ^ hashed >> 15
    hashed = hashed * 747796405
    hashed = hashed ^ hashed >> 13
    bit_value = hashed >> 7 & 1
    return (2 * bit_value - 1).astype(jnp.bfloat16)

def example_feature(grad_rows, act_rows, mark_rows, scaling, signs_table, inv_root):
    masked = act_rows * mark_rows[:, None]
    outer_sum = jnp.dot(grad_rows.T, masked, preferred_element_type=jnp.float32)
    scaled = (outer_sum / scaling).astype(jnp.bfloat16)
    projected = jnp.dot(signs_table.T, scaled, preferred_element_type=jnp.float32) * inv_root
    return projected.astype(jnp.bfloat16).reshape(-1)

def reference(output_gradient, adapter_activation, adaptive_variance, holdout_feature, lengths, token_loss_mask, sketch_seed, step_size_weight):
    positions = jnp.arange(TOKEN_SLOTS, dtype=jnp.int32)[None, :]
    valid_marks = ((token_loss_mask == 1) & (positions < lengths[:, None])).astype(jnp.bfloat16)
    seed_value = sketch_seed[0]
    inv_root = 1.0 / math.sqrt(D)
    scores = jnp.zeros((TRAIN_SAMPLES, NVAL), jnp.float32)
    for snapshot_index in range(SAVED_POINTS):

        def layerwise_result(totals, layer_items):
            common_part, squared_norm = totals
            grad_block, act_block, moment, val_block, layer_id = layer_items
            signs_table = projection(seed_value, layer_id, D, KL)
            scaling = jnp.sqrt(moment.astype(jnp.float32)) + 1e-08

            def one_example(example_items):
                return example_feature(example_items[0], example_items[1], example_items[2], scaling, signs_table, inv_root)
            features = lax.map(one_example, (grad_block, act_block, valid_marks))
            common_part = common_part + jnp.dot(features, val_block.T, preferred_element_type=jnp.float32)
            wide_features = features.astype(jnp.float32)
            squared_norm = squared_norm + lax.optimization_barrier(jnp.sum(wide_features * wide_features, axis=1))
            return ((common_part, squared_norm), None)
        starting_value = (jnp.zeros((TRAIN_SAMPLES, NVAL), jnp.float32), jnp.zeros((TRAIN_SAMPLES,), jnp.float32))
        layer_numbers = jnp.arange(MODEL_LAYERS, dtype=jnp.int32)
        (common_part, squared_norm), ignored_value = lax.scan(layerwise_result, starting_value, (output_gradient[snapshot_index], adapter_activation[snapshot_index], adaptive_variance[snapshot_index], holdout_feature[snapshot_index], layer_numbers))
        scores = scores + step_size_weight[snapshot_index] * common_part * lax.rsqrt(squared_norm + 1e-06)[:, None]
    return scores
```

```python
import functools
import math

import jax
import jax.numpy as jnp
from jax import lax
from jax.experimental import pallas as pl
from jax.experimental.pallas import tpu as pltpu
from jax.sharding import PartitionSpec as P

F32 = jnp.float32
BF16 = jnp.bfloat16
TILE = 256
LANES = 128
AHEAD = 2


def feature_kernel(
    seed_ref,
    len_ref,
    mask_ref,
    act_ref,
    grad_hbm,
    var_hbm,
    out_ref,
    grad_raw,
    var_raw,
    lhs_ring,
    scale_ring,
    sign_ring,
    act_blocks,
    feat_buf,
    sems,
    *,
    ckpts,
    examples,
    slots,
    width,
    cols,
    tiles,
):
    chunk = tiles * TILE
    chunks = width // chunk
    total = ckpts * chunks
    rows = examples * slots
    pairs = examples // 2
    per_unit = pairs // 2
    sign_rows = sign_ring.shape[0]
    inv_root = 1.0 / math.sqrt(width)

    def copies(it):
        c, q = it // chunks, it % chunks
        at = pl.ds(pl.multiple_of(q * chunk, chunk), chunk)
        return (
            pltpu.make_async_copy(grad_hbm.at[c, :, at], grad_raw.at[c, :, at], sems.at[0, it]),
            pltpu.make_async_copy(var_hbm.at[c, at, :], var_raw.at[c, at, :], sems.at[1, it]),
        )

    for it in range(total):
        for copy in copies(it):
            copy.start()

    hash_base = (
        lax.axis_index("layer") * jnp.int32(668265263) + seed_ref[0] * jnp.int32(374761393)
    )

    act_blocks[...] = jnp.zeros_like(act_blocks)
    lhs_ring[:, LANES:] = jnp.zeros((chunk, TILE - LANES), BF16)
    slot_ids = lax.broadcasted_iota(jnp.int32, (slots, slots), 0)
    diagonal = slot_ids == lax.broadcasted_iota(jnp.int32, (slots, slots), 1)
    for pair in range(pairs):
        marks = []
        for e in (2 * pair, 2 * pair + 1):
            spread = jnp.where(diagonal, jnp.broadcast_to(mask_ref[e : e + 1, :], (slots, slots)), 0)
            marked = jnp.sum(spread.astype(F32), axis=1, keepdims=True) == 1.0
            marks.append(marked & (slot_ids[:, :1] < len_ref[e]))
        for c in range(ckpts):
            at = 2 * pair * slots
            first = jnp.where(marks[0], act_ref[c, at : at + slots, :].astype(F32), 0.0)
            second = jnp.where(marks[1], act_ref[c, at + slots : at + 2 * slots, :].astype(F32), 0.0)
            blank = jnp.zeros_like(first)
            act_blocks[c * pairs + pair, at : at + 2 * slots, :] = jnp.concatenate(
                [jnp.concatenate([first, blank], 1), jnp.concatenate([blank, second], 1)], 0
            ).astype(BF16)

    def prepare(it, t, part):
        c, q = it // chunks, it % chunks
        base = q * chunk + t * TILE
        here = t * TILE
        if part < 2:
            half = part * LANES
            src = grad_raw[c, :, pl.ds(pl.multiple_of(base + half, LANES), LANES)]
            lhs_ring[here + half : here + half + LANES, :LANES] = jnp.transpose(src)
        elif part == 2:
            moment = var_raw[c, pl.ds(pl.multiple_of(base, TILE), TILE), :].astype(F32)
            scale_ring[here : here + TILE, :] = 1.0 / (jnp.sqrt(moment) + 1e-08)
        else:
            d = lax.broadcasted_iota(jnp.int32, (sign_rows, TILE), 1) + base
            k = lax.broadcasted_iota(jnp.int32, (sign_rows, TILE), 0)
            m = d * jnp.int32(1103515245) + k * jnp.int32(12345) + hash_base
            m = m ^ (m >> 15)
            m = m * jnp.int32(747796405)
            m = m ^ (m >> 13)
            sign = (2 * ((m >> 7) & 1) - 1).astype(F32)
            sign_ring[:, here : here + TILE] = jnp.where(k < cols, sign, 0.0).astype(BF16)

    for copy in copies(0):
        copy.wait()
    for t in range(tiles - 1):
        for part in range(4):
            prepare(0, t, part)

    def scoped(*accs):
        depth = AHEAD + 1
        outer_acc = [accs[m * depth : (m + 1) * depth] for m in (0, 1)]
        proj_acc = [accs[2 * depth + m * per_unit : 2 * depth + (m + 1) * per_unit] for m in (0, 1)]
        steps = [(t, j) for t in range(tiles) for j in range(per_unit)]

        def outer(c, m, n):
            t, j = steps[n]
            pltpu.matmul_push_rhs(act_blocks[c * pairs + m * per_unit + j], 0, m)
            pltpu.matmul_acc_lhs(
                outer_acc[m][n % depth], lhs_ring[t * TILE : (t + 1) * TILE, :], load_staged_rhs=0
            )

        def project(m, n):
            t, j = steps[n]
            at = slice(t * TILE, (t + 1) * TILE)
            summed = pltpu.matmul_pop(outer_acc[m][n % depth])
            scale = scale_ring[at, :]
            scaled = (summed * jnp.concatenate([scale, scale], 1)).astype(BF16)
            pltpu.matmul_push_rhs(scaled, 1, m)
            pltpu.matmul_acc_lhs(proj_acc[m][j], sign_ring[:, at], load_staged_rhs=1)

        def one_chunk(c, q):
            it = c * chunks + q
            following = jnp.minimum(it + 1, total - 1)

            @pl.when(it + 1 < total)
            def _():
                for copy in copies(it + 1):
                    copy.wait()

            for n in range(AHEAD):
                for m in (0, 1):
                    outer(c, m, n)
            for n in range(len(steps)):
                for m in (0, 1):
                    if n + AHEAD < len(steps):
                        outer(c, m, n + AHEAD)
                    project(m, n)
                t, j = steps[n]
                for part in range(j * 4 // per_unit, (j + 1) * 4 // per_unit):
                    if t == 0:
                        prepare(it, tiles - 1, part)
                    else:
                        prepare(following, t - 1, part)

        def one_ckpt(c, carry):
            def body(q, inner):
                one_chunk(c, q)
                return inner

            lax.fori_loop(0, chunks, body, 0)
            for m in (0, 1):
                for j in range(per_unit):
                    total_sum = pltpu.matmul_pop(proj_acc[m][j])
                    for half in range(2):
                        e = 2 * (m * per_unit + j) + half
                        feat_buf[e] = total_sum[:cols, half * LANES : (half + 1) * LANES] * inv_root
            for k in range(cols):
                out_ref[c, :, k * LANES : (k + 1) * LANES] = feat_buf[:, k, :].astype(BF16)
            return carry

        lax.fori_loop(0, ckpts, one_ckpt, 0)

    pl.run_scoped(
        scoped,
        *[pltpu.ACC(m)((TILE, TILE), F32) for m in (0, 1) for _ in range(AHEAD + 1)],
        *[pltpu.ACC(m)((sign_rows, TILE), F32) for m in (0, 1) for _ in range(per_unit)],
    )


def features_of(seed, lengths, mask, act, grad, var, cols):
    ckpts, rows, width = grad.shape
    examples, slots = mask.shape
    tiles = 8
    chunk = tiles * TILE
    pairs = examples // 2
    sign_rows = -(-cols // 16) * 16
    vmem = pl.BlockSpec(memory_space=pltpu.VMEM)
    smem = pl.BlockSpec(memory_space=pltpu.SMEM)
    hbm = pl.BlockSpec(memory_space=pl.ANY)
    kernel = functools.partial(
        feature_kernel,
        ckpts=ckpts,
        examples=examples,
        slots=slots,
        width=width,
        cols=cols,
        tiles=tiles,
    )
    return pl.pallas_call(
        kernel,
        out_shape=jax.ShapeDtypeStruct((ckpts, examples, cols * LANES), BF16),
        in_specs=[smem, smem, vmem, vmem, hbm, hbm],
        out_specs=vmem,
        scratch_shapes=[
            pltpu.VMEM((ckpts, rows, width), BF16),
            pltpu.VMEM((ckpts, width, LANES), BF16),
            pltpu.VMEM((chunk, TILE), BF16),
            pltpu.VMEM((chunk, LANES), F32),
            pltpu.VMEM((sign_rows, chunk), BF16),
            pltpu.VMEM((ckpts * pairs, TILE, TILE), BF16),
            pltpu.VMEM((examples, cols, LANES), F32),
            pltpu.SemaphoreType.DMA((2, ckpts * width // chunk)),
        ],
        compiler_params=pltpu.CompilerParams(vmem_limit_bytes=40 << 20),
        cost_estimate=pl.CostEstimate(
            flops=40_000_000_000, bytes_accessed=9_000_000, transcendentals=0
        ),
        name="features",
    )(seed, lengths, mask, act, grad, var)


def score_kernel(feat_ref, hold_ref, out_ref, sums, *, parts):
    ckpts, examples, _ = feat_ref.shape
    held = hold_ref.shape[1]
    share = examples // parts
    me = lax.axis_index("layer")
    for c in range(ckpts):
        feat = feat_ref[c]
        sums[c, :, :held] = lax.dot_general(
            feat, hold_ref[c], (((1,), (1,)), ((), ())), preferred_element_type=F32
        )
        wide = feat.astype(F32)
        norm = jnp.sum(wide * wide, axis=1, keepdims=True)
        sums[c, :, held:] = jnp.broadcast_to(norm, (examples, sums.shape[2] - held))
        for step in range(parts):
            owner = lax.rem(me + step, parts)
            out_ref[step, c] = sums[c, pl.ds(owner * share, share), :]


def scores_of(feat, hold, parts):
    ckpts, examples, _ = feat.shape
    held = hold.shape[1]
    lanes = (held // LANES + 1) * LANES
    vmem = pl.BlockSpec(memory_space=pltpu.VMEM)
    return pl.pallas_call(
        functools.partial(score_kernel, parts=parts),
        out_shape=jax.ShapeDtypeStruct((parts, ckpts, examples // parts, lanes), F32),
        in_specs=[vmem, vmem],
        out_specs=vmem,
        scratch_shapes=[pltpu.VMEM((ckpts, examples, lanes), F32)],
        name="scores",
    )(feat, hold)


def solution(mesh):
    parts = mesh.shape["layer"]

    def local(grad, act, var, hold, lengths, mask, seed, weight):
        ckpts, _, examples, slots, width = grad.shape
        rank = act.shape[-1]
        cols = hold.shape[-1] // rank
        everyone = lax.all_gather(hold[:, 0], "dp", axis=1, tiled=True)
        feat = features_of(
            seed,
            lengths,
            mask,
            act.reshape(ckpts, examples * slots, rank),
            grad.reshape(ckpts, examples * slots, width),
            var[:, 0],
            cols,
        )
        pieces = scores_of(feat, everyone, parts)
        total = pieces[0]
        for step in range(1, parts):
            total = total + lax.ppermute(
                pieces[step], "layer", [(i, (i + step) % parts) for i in range(parts)]
            )
        held = everyone.shape[1]
        common, norm = total[:, :, :held], total[:, :, held : held + 1]
        return jnp.sum(weight[:, None, None] * common * lax.rsqrt(norm + 1e-06), axis=0)

    placed = (
        P(None, "layer", "dp", None, None),
        P(None, "layer", "dp", None, None),
        P(None, "layer", None, None),
        P(None, "layer", "dp", None),
        P("dp"),
        P("dp", None),
        P(),
        P(),
    )
    return jax.shard_map(
        local, mesh=mesh, in_specs=placed, out_specs=P(("dp", "layer"), None), check_vma=False
    )
```

```python
import functools
import math

import jax
import jax.numpy as jnp
from jax import lax
from jax.experimental import pallas as pl
from jax.experimental.pallas import tpu as pltpu
from jax.sharding import PartitionSpec as P

F32 = jnp.float32
BF16 = jnp.bfloat16
TILE = 256
LANES = 128
AHEAD = 2


def feature_kernel(
    seed_hbm,
    len_hbm,
    mask_hbm,
    act_hbm,
    grad_hbm,
    var_hbm,
    out_ref,
    seed_ref,
    len_ref,
    mask_ref,
    act_ref,
    grad_raw,
    var_raw,
    lhs_ring,
    scale_ring,
    sign_ring,
    act_blocks,
    feat_buf,
    small_sems,
    sems,
    *,
    ckpts,
    examples,
    slots,
    width,
    cols,
    tiles,
):
    chunk = tiles * TILE
    chunks = width // chunk
    total = ckpts * chunks
    rows = examples * slots
    pairs = examples // 2
    per_unit = pairs // 2
    sign_rows = sign_ring.shape[0]
    inv_root = 1.0 / math.sqrt(width)

    def copies(it):
        c, q = it // chunks, it % chunks
        at = pl.ds(pl.multiple_of(q * chunk, chunk), chunk)
        return (
            pltpu.make_async_copy(grad_hbm.at[c, :, at], grad_raw.at[c, :, at], sems.at[0, it]),
            pltpu.make_async_copy(var_hbm.at[c, at, :], var_raw.at[c, at, :], sems.at[1, it]),
        )

    small = [
        pltpu.make_async_copy(src, dst, small_sems.at[i])
        for i, (src, dst) in enumerate(
            (
                (seed_hbm, seed_ref),
                (len_hbm, len_ref),
                (mask_hbm, mask_ref),
                (act_hbm, act_ref),
            )
        )
    ]
    for copy in small:
        copy.start()
    for it in range(total):
        for copy in copies(it):
            copy.start()
    act_blocks[...] = jnp.zeros_like(act_blocks)
    lhs_ring[:, LANES:] = jnp.zeros((chunk, TILE - LANES), BF16)
    for copy in small:
        copy.wait()

    hash_base = (
        lax.axis_index("layer") * jnp.int32(668265263) + seed_ref[0] * jnp.int32(374761393)
    )

    slot_ids = lax.broadcasted_iota(jnp.int32, (slots, 1), 0)
    for pair in range(pairs):
        marks = [
            (mask_ref[:, e : e + 1] == 1) & (slot_ids < len_ref[e])
            for e in (2 * pair, 2 * pair + 1)
        ]
        for c in range(ckpts):
            at = 2 * pair * slots
            first = jnp.where(marks[0], act_ref[c, at : at + slots, :].astype(F32), 0.0)
            second = jnp.where(marks[1], act_ref[c, at + slots : at + 2 * slots, :].astype(F32), 0.0)
            blank = jnp.zeros_like(first)
            act_blocks[c * pairs + pair, at : at + 2 * slots, :] = jnp.concatenate(
                [jnp.concatenate([first, blank], 1), jnp.concatenate([blank, second], 1)], 0
            ).astype(BF16)

    def prepare(it, t, part):
        c, q = it // chunks, it % chunks
        base = q * chunk + t * TILE
        here = t * TILE
        if part < 2:
            half = part * LANES
            src = grad_raw[c, :, pl.ds(pl.multiple_of(base + half, LANES), LANES)]
            lhs_ring[here + half : here + half + LANES, :LANES] = jnp.transpose(src)
        elif part == 2:
            moment = var_raw[c, pl.ds(pl.multiple_of(base, TILE), TILE), :].astype(F32)
            scale_ring[here : here + TILE, :] = 1.0 / (jnp.sqrt(moment) + 1e-08)
        else:
            d = lax.broadcasted_iota(jnp.int32, (sign_rows, TILE), 1) + base
            k = lax.broadcasted_iota(jnp.int32, (sign_rows, TILE), 0)
            m = d * jnp.int32(1103515245) + k * jnp.int32(12345) + hash_base
            m = m ^ (m >> 15)
            m = m * jnp.int32(747796405)
            m = m ^ (m >> 13)
            sign = (2 * ((m >> 7) & 1) - 1).astype(F32)
            sign_ring[:, here : here + TILE] = jnp.where(k < cols, sign, 0.0).astype(BF16)

    for copy in copies(0):
        copy.wait()
    for t in range(tiles - 1):
        for part in range(4):
            prepare(0, t, part)

    def scoped(*accs):
        depth = AHEAD + 1
        outer_acc = [accs[m * depth : (m + 1) * depth] for m in (0, 1)]
        proj_acc = [accs[2 * depth + m * per_unit : 2 * depth + (m + 1) * per_unit] for m in (0, 1)]
        steps = [(t, j) for t in range(tiles) for j in range(per_unit)]

        def outer(c, m, n):
            t, j = steps[n]
            pltpu.matmul_push_rhs(act_blocks[c * pairs + m * per_unit + j], 0, m)
            pltpu.matmul_acc_lhs(
                outer_acc[m][n % depth], lhs_ring[t * TILE : (t + 1) * TILE, :], load_staged_rhs=0
            )

        def project(m, n):
            t, j = steps[n]
            at = slice(t * TILE, (t + 1) * TILE)
            summed = pltpu.matmul_pop(outer_acc[m][n % depth])
            scale = scale_ring[at, :]
            scaled = (summed * jnp.concatenate([scale, scale], 1)).astype(BF16)
            pltpu.matmul_push_rhs(scaled, 1, m)
            pltpu.matmul_acc_lhs(proj_acc[m][j], sign_ring[:, at], load_staged_rhs=1)

        def one_chunk(c, q):
            it = c * chunks + q
            following = jnp.minimum(it + 1, total - 1)

            @pl.when(it + 1 < total)
            def _():
                for copy in copies(it + 1):
                    copy.wait()

            for n in range(AHEAD):
                for m in (0, 1):
                    outer(c, m, n)
            for n in range(len(steps)):
                for m in (0, 1):
                    if n + AHEAD < len(steps):
                        outer(c, m, n + AHEAD)
                    project(m, n)
                t, j = steps[n]
                for part in range(j * 4 // per_unit, (j + 1) * 4 // per_unit):
                    if t == 0:
                        prepare(it, tiles - 1, part)
                    else:
                        prepare(following, t - 1, part)

        def one_ckpt(c, carry):
            def body(q, inner):
                one_chunk(c, q)
                return inner

            lax.fori_loop(0, chunks, body, 0)
            for m in (0, 1):
                for j in range(per_unit):
                    total_sum = pltpu.matmul_pop(proj_acc[m][j])
                    for half in range(2):
                        e = 2 * (m * per_unit + j) + half
                        feat_buf[e] = total_sum[:cols, half * LANES : (half + 1) * LANES] * inv_root
            for k in range(cols):
                out_ref[c, :, k * LANES : (k + 1) * LANES] = feat_buf[:, k, :].astype(BF16)
            return carry

        lax.fori_loop(0, ckpts, one_ckpt, 0)

    pl.run_scoped(
        scoped,
        *[pltpu.ACC(m)((TILE, TILE), F32) for m in (0, 1) for _ in range(AHEAD + 1)],
        *[pltpu.ACC(m)((sign_rows, TILE), F32) for m in (0, 1) for _ in range(per_unit)],
    )


def features_of(seed, lengths, mask, act, grad, var, cols):
    ckpts, rows, width = grad.shape
    slots, examples = mask.shape
    tiles = 8
    chunk = tiles * TILE
    pairs = examples // 2
    sign_rows = -(-cols // 16) * 16
    vmem = pl.BlockSpec(memory_space=pltpu.VMEM)
    hbm = pl.BlockSpec(memory_space=pltpu.HBM)
    kernel = functools.partial(
        feature_kernel,
        ckpts=ckpts,
        examples=examples,
        slots=slots,
        width=width,
        cols=cols,
        tiles=tiles,
    )
    return pl.pallas_call(
        kernel,
        out_shape=jax.ShapeDtypeStruct((ckpts, examples, cols * LANES), BF16),
        in_specs=[hbm] * 6,
        out_specs=vmem,
        scratch_shapes=[
            pltpu.SMEM(seed.shape, jnp.int32),
            pltpu.SMEM(lengths.shape, jnp.int32),
            pltpu.VMEM(mask.shape, jnp.int32),
            pltpu.VMEM(act.shape, BF16),
            pltpu.VMEM((ckpts, rows, width), BF16),
            pltpu.VMEM((ckpts, width, LANES), BF16),
            pltpu.VMEM((chunk, TILE), BF16),
            pltpu.VMEM((chunk, LANES), F32),
            pltpu.VMEM((sign_rows, chunk), BF16),
            pltpu.VMEM((ckpts * pairs, TILE, TILE), BF16),
            pltpu.VMEM((examples, cols, LANES), F32),
            pltpu.SemaphoreType.DMA((4,)),
            pltpu.SemaphoreType.DMA((2, ckpts * width // chunk)),
        ],
        compiler_params=pltpu.CompilerParams(vmem_limit_bytes=57 << 20),
        cost_estimate=pl.CostEstimate(
            flops=40_000_000_000, bytes_accessed=9_000_000, transcendentals=0
        ),
        name="features",
    )(seed, lengths, mask, act, grad, var)


def score_kernel(*refs, groups, parts):
    feat_ref, holds, outs = refs[0], refs[1 : 1 + groups], refs[1 + groups : 1 + groups + parts]
    hold_ref, sums, sems = refs[1 + groups + parts :]
    ckpts, examples, width = feat_ref.shape
    peers, block = hold_ref.shape[1:3]
    members = peers // groups
    held = peers * block
    share = examples // parts
    mine = lax.axis_index("dp")
    me = lax.axis_index("layer")
    group, member = mine // members, lax.rem(mine, members)
    copies = []
    for step in range(groups):
        source = lax.rem(group + groups - step, groups) * members
        for turn in range(members):
            index = source + lax.rem(member + turn, members)
            copies.append(
                pltpu.make_async_copy(
                    holds[step].at[:, turn], hold_ref.at[:, index], sems.at[step, turn]
                )
            )
    for copy in copies:
        copy.start()
    for c in range(ckpts):
        wide = feat_ref[c].astype(F32)
        norm = jnp.sum(wide * wide, axis=1, keepdims=True)
        sums[c, :, held:] = jnp.broadcast_to(norm, (examples, sums.shape[2] - held))
    for copy in copies:
        copy.wait()
    for c in range(ckpts):
        sums[c, :, :held] = lax.dot_general(
            feat_ref[c],
            hold_ref[c].reshape(held, width),
            (((1,), (1,)), ((), ())),
            preferred_element_type=F32,
        )
        for step in range(parts):
            owner = lax.rem(me + step, parts)
            outs[step][c] = sums[c, pl.ds(owner * share, share), :]


def scores_of(feat, holds, parts):
    ckpts, examples, width = feat.shape
    groups = len(holds)
    members, block = holds[0].shape[1:3]
    peers = groups * members
    lanes = (peers * block // LANES + 1) * LANES
    vmem = pl.BlockSpec(memory_space=pltpu.VMEM)
    anywhere = pl.BlockSpec(memory_space=pl.ANY)
    return pl.pallas_call(
        functools.partial(score_kernel, groups=groups, parts=parts),
        out_shape=[jax.ShapeDtypeStruct((ckpts, examples // parts, lanes), F32)] * parts,
        in_specs=[vmem] + [anywhere] * groups,
        out_specs=[vmem] * parts,
        scratch_shapes=[
            pltpu.VMEM((ckpts, peers, block, width), BF16),
            pltpu.VMEM((ckpts, examples, lanes), F32),
            pltpu.SemaphoreType.DMA((groups, members)),
        ],
        compiler_params=pltpu.CompilerParams(vmem_limit_bytes=12 << 20),
        name="scores",
    )(feat, *holds)


def finish_kernel(*refs):
    weight_ref, pieces, out_ref = refs[0], refs[1:-1], refs[-1]
    held = out_ref.shape[1]
    result = jnp.zeros(out_ref.shape, F32)
    for c in range(pieces[0].shape[0]):
        total = pieces[0][c]
        for piece in pieces[1:]:
            total = total + piece[c]
        scale = weight_ref[c] * lax.rsqrt(total[:, held : held + 1] + 1e-06)
        result = result + total[:, :held] * scale
    out_ref[...] = result


def solution(mesh):
    parts = mesh.shape["layer"]
    peers = mesh.shape["dp"]

    def local(grad, act, var, hold, lengths, mask, seed, weight):
        ckpts, _, examples, slots, width = grad.shape
        rank = act.shape[-1]
        cols = hold.shape[-1] // rank
        members = 2 if peers % 2 == 0 else 1
        groups = peers // members
        gathered = [hold[:, 0]]
        for turn in range(1, members):
            ring = [
                (i, i // members * members + (i + members - turn) % members) for i in range(peers)
            ]
            gathered.append(lax.ppermute(hold[:, 0], "dp", ring))
        own = jnp.stack(gathered, axis=1)
        holds = [own]
        for step in range(1, groups):
            ring = [(i, (i + step * members) % peers) for i in range(peers)]
            holds.append(lax.ppermute(own, "dp", ring))
        feat = features_of(
            seed,
            lengths,
            mask.T,
            act.reshape(ckpts, examples * slots, rank),
            grad.reshape(ckpts, examples * slots, width),
            var[:, 0],
            cols,
        )
        pieces = list(scores_of(feat, holds, parts))
        for step in range(1, parts):
            ring = [(i, (i + step) % parts) for i in range(parts)]
            pieces[step] = lax.ppermute(pieces[step], "layer", ring)
        vmem = pl.BlockSpec(memory_space=pltpu.VMEM)
        return pl.pallas_call(
            finish_kernel,
            out_shape=jax.ShapeDtypeStruct((examples // parts, peers * hold.shape[2]), F32),
            in_specs=[pl.BlockSpec(memory_space=pltpu.SMEM)] + [vmem] * parts,
            out_specs=vmem,
            compiler_params=pltpu.CompilerParams(vmem_limit_bytes=12 << 20),
            name="finish",
        )(weight, *pieces)

    placed = (
        P(None, "layer", "dp", None, None),
        P(None, "layer", "dp", None, None),
        P(None, "layer", None, None),
        P(None, "layer", "dp", None),
        P("dp"),
        P("dp", None),
        P(),
        P(),
    )
    return jax.shard_map(
        local, mesh=mesh, in_specs=placed, out_specs=P(("dp", "layer"), None), check_vma=False
    )
```

```python
import functools
import math

import jax
import jax.numpy as jnp
from jax import lax
from jax.experimental import pallas as pl
from jax.experimental.pallas import tpu as pltpu
from jax.sharding import PartitionSpec as P

F32 = jnp.float32
BF16 = jnp.bfloat16
TILE = 256
LANES = 128
AHEAD = 2
READY = 2


def feature_kernel(
    seed_hbm,
    len_hbm,
    mask_hbm,
    act_hbm,
    grad_hbm,
    var_hbm,
    out_ref,
    seed_ref,
    len_ref,
    mask_ref,
    act_ref,
    grad_raw,
    var_raw,
    lhs_ring,
    scale_ring,
    sign_ring,
    act_blocks,
    feat_buf,
    small_sems,
    grad_sems,
    var_sems,
    *,
    ckpts,
    examples,
    slots,
    width,
    cols,
    tiles,
):
    chunk = tiles * TILE
    chunks = width // chunk
    total = ckpts * chunks
    pairs = examples // 2
    per_unit = pairs // 2
    sign_rows = sign_ring.shape[0]
    inv_root = 1.0 / math.sqrt(width)

    def copies(it):
        c, q = it // chunks, it % chunks
        at = pl.ds(pl.multiple_of(q * chunk, chunk), chunk)
        return (
            pltpu.make_async_copy(grad_hbm.at[c, :, at], grad_raw.at[c, :, at], grad_sems.at[it]),
            pltpu.make_async_copy(var_hbm.at[c, at, :], var_raw.at[c, at, :], var_sems.at[it]),
        )


    small = [
        pltpu.make_async_copy(src, dst, small_sems.at[i])
        for i, (src, dst) in enumerate(
            (
                (seed_hbm, seed_ref),
                (len_hbm, len_ref),
                (mask_hbm, mask_ref),
                (act_hbm, act_ref),
            )
        )
    ]
    for copy in (*copies(0), *small, *copies(1)):
        copy.start()
    act_blocks[...] = jnp.zeros_like(act_blocks)
    for copy in small:
        copy.wait()
    hash_base = (
        lax.axis_index("layer") * jnp.int32(668265263) + seed_ref[0] * jnp.int32(374761393)
    )
    slot_ids = lax.broadcasted_iota(jnp.int32, (slots, 1), 0)

    for pair in range(pairs):
        marks = [
            (mask_ref[:, e : e + 1] == 1) & (slot_ids < len_ref[e])
            for e in (2 * pair, 2 * pair + 1)
        ]
        for c in range(ckpts):
            at = 2 * pair * slots
            first = jnp.where(marks[0], act_ref[c, at : at + slots, :].astype(F32), 0.0)
            second = jnp.where(marks[1], act_ref[c, at + slots : at + 2 * slots, :].astype(F32), 0.0)
            blank = jnp.zeros_like(first)
            act_blocks[c * pairs + pair, at : at + 2 * slots, :] = jnp.concatenate(
                [jnp.concatenate([first, blank], 1), jnp.concatenate([blank, second], 1)], 0
            ).astype(BF16)

    def prepare(it, t, part):
        c, q = it // chunks, it % chunks
        base = q * chunk + t * TILE
        here = t * TILE
        if part < 2:
            half = part * LANES
            src = grad_raw[c, :, pl.ds(pl.multiple_of(base + half, LANES), LANES)]
            lhs_ring[here + half : here + half + LANES, :] = jnp.transpose(src)
        elif part == 2:
            moment = var_raw[c, pl.ds(pl.multiple_of(base, TILE), TILE), :].astype(F32)
            scale_ring[here : here + TILE, :] = 1.0 / (jnp.sqrt(moment) + 1e-08)
        else:
            d = lax.broadcasted_iota(jnp.int32, (sign_rows, TILE), 1) + base
            k = lax.broadcasted_iota(jnp.int32, (sign_rows, TILE), 0)
            m = d * jnp.int32(1103515245) + k * jnp.int32(12345) + hash_base
            m = m ^ (m >> 15)
            m = m * jnp.int32(747796405)
            m = m ^ (m >> 13)
            sign = (2 * ((m >> 7) & 1) - 1).astype(F32)
            sign_ring[:, here : here + TILE] = jnp.where(k < cols, sign, 0.0).astype(BF16)

    for copy in copies(0):
        copy.wait()
    for it in range(2, total):
        for copy in copies(it):
            copy.start()
    for t in range(READY):
        for part in range(4):
            prepare(0, t, part)

    def scoped(*accs):
        depth = AHEAD + 1
        outer_acc = [accs[m * depth : (m + 1) * depth] for m in (0, 1)]
        proj_acc = [accs[2 * depth + m * per_unit : 2 * depth + (m + 1) * per_unit] for m in (0, 1)]
        steps = [(t, j) for t in range(tiles) for j in range(per_unit)]

        def outer(c, m, n):
            t, j = steps[n]
            tokens = lhs_ring[t * TILE : (t + 1) * TILE, :]
            pltpu.matmul_push_rhs(act_blocks[c * pairs + m * per_unit + j], 0, m)
            pltpu.matmul_acc_lhs(
                outer_acc[m][n % depth], jnp.concatenate([tokens, tokens], 1), load_staged_rhs=0
            )

        def project(m, n):
            t, j = steps[n]
            at = slice(t * TILE, (t + 1) * TILE)
            summed = pltpu.matmul_pop(outer_acc[m][n % depth])
            scale = scale_ring[at, :]
            scaled = (summed * jnp.concatenate([scale, scale], 1)).astype(BF16)
            pltpu.matmul_push_rhs(scaled, 1, m)
            pltpu.matmul_acc_lhs(proj_acc[m][j], sign_ring[:, at], load_staged_rhs=1)

        def one_chunk(c, q):
            it = c * chunks + q
            following = jnp.minimum(it + 1, total - 1)

            @pl.when(it + 1 < total)
            def _():
                for copy in copies(it + 1):
                    copy.wait()

            for n in range(1, AHEAD):
                for m in (0, 1):
                    outer(c, m, n)
            for n in range(len(steps)):
                for m in (0, 1):
                    if n + AHEAD < len(steps):
                        outer(c, m, n + AHEAD)
                    project(m, n)
                    if n == len(steps) - 2:
                        outer(following // chunks, m, 0)
                t, j = steps[n]
                for part in range(j * 4 // per_unit, (j + 1) * 4 // per_unit):
                    if t + READY < tiles:
                        prepare(it, t + READY, part)
                    else:
                        prepare(following, t + READY - tiles, part)

        def one_ckpt(c, carry):
            def body(q, inner):
                one_chunk(c, q)
                return inner

            lax.fori_loop(0, chunks, body, 0)
            for m in (0, 1):
                for j in range(per_unit):
                    total_sum = pltpu.matmul_pop(proj_acc[m][j])
                    for half in range(2):
                        e = 2 * (m * per_unit + j) + half
                        feat_buf[e] = total_sum[:cols, half * LANES : (half + 1) * LANES] * inv_root
            for k in range(cols):
                out_ref[c, :, k * LANES : (k + 1) * LANES] = feat_buf[:, k, :].astype(BF16)
            return carry

        for m in (0, 1):
            outer(0, m, 0)
        lax.fori_loop(0, ckpts, one_ckpt, 0)
        for m in (0, 1):
            pltpu.matmul_pop(outer_acc[m][0])

    pl.run_scoped(
        scoped,
        *[pltpu.ACC(m)((TILE, TILE), F32) for m in (0, 1) for _ in range(AHEAD + 1)],
        *[pltpu.ACC(m)((sign_rows, TILE), F32) for m in (0, 1) for _ in range(per_unit)],
    )


def features_of(seed, lengths, mask, act, grad, var, cols):
    ckpts, rows, width = grad.shape
    slots, examples = mask.shape
    tiles = 8
    chunk = tiles * TILE
    pairs = examples // 2
    sign_rows = -(-cols // 16) * 16
    vmem = pl.BlockSpec(memory_space=pltpu.VMEM)
    hbm = pl.BlockSpec(memory_space=pltpu.HBM)
    kernel = functools.partial(
        feature_kernel,
        ckpts=ckpts,
        examples=examples,
        slots=slots,
        width=width,
        cols=cols,
        tiles=tiles,
    )
    return pl.pallas_call(
        kernel,
        out_shape=jax.ShapeDtypeStruct((ckpts, examples, cols * LANES), BF16),
        in_specs=[hbm] * 6,
        out_specs=vmem,
        scratch_shapes=[
            pltpu.SMEM(seed.shape, jnp.int32),
            pltpu.SMEM(lengths.shape, jnp.int32),
            pltpu.VMEM(mask.shape, jnp.int32),
            pltpu.VMEM(act.shape, BF16),
            pltpu.VMEM((ckpts, rows, width), BF16),
            pltpu.VMEM((ckpts, width, LANES), BF16),
            pltpu.VMEM((chunk, LANES), BF16),
            pltpu.VMEM((chunk, LANES), F32),
            pltpu.VMEM((sign_rows, chunk), BF16),
            pltpu.VMEM((ckpts * pairs, TILE, TILE), BF16),
            pltpu.VMEM((examples, cols, LANES), F32),
            pltpu.SemaphoreType.DMA((4,)),
            pltpu.SemaphoreType.DMA((ckpts * width // chunk,)),
            pltpu.SemaphoreType.DMA((ckpts * width // chunk,)),
        ],
        compiler_params=pltpu.CompilerParams(vmem_limit_bytes=57 << 20),
        cost_estimate=pl.CostEstimate(
            flops=40_000_000_000, bytes_accessed=9_000_000, transcendentals=0
        ),
        name="features",
    )(seed, lengths, mask, act, grad, var)


def score_kernel(*refs, groups, parts):
    feat_hbm, holds, outs = refs[0], refs[1 : 1 + groups], refs[1 + groups : 1 + groups + parts]
    feat_ref, hold_ref, sums, sems, feat_sem = refs[1 + groups + parts :]
    feat_copy = pltpu.make_async_copy(feat_hbm, feat_ref, feat_sem)
    feat_copy.start()
    ckpts, examples, width = feat_ref.shape
    peers, block = hold_ref.shape[1:3]
    members = peers // groups
    held = peers * block
    share = examples // parts
    mine = lax.axis_index("dp")
    me = lax.axis_index("layer")
    group, member = mine // members, lax.rem(mine, members)
    copies = []
    for step in range(groups):
        source = lax.rem(group + groups - step, groups) * members
        for turn in range(members):
            index = source + lax.rem(member + turn, members)
            copies.append(
                pltpu.make_async_copy(
                    holds[step].at[:, turn], hold_ref.at[:, index], sems.at[step, turn]
                )
            )
    for copy in copies:
        copy.start()
    feat_copy.wait()
    for c in range(ckpts):
        wide = feat_ref[c].astype(F32)
        norm = jnp.sum(wide * wide, axis=1, keepdims=True)
        sums[c, :, held:] = jnp.broadcast_to(norm, (examples, sums.shape[2] - held))
    for copy in copies:
        copy.wait()
    for c in range(ckpts):
        sums[c, :, :held] = lax.dot_general(
            feat_ref[c],
            hold_ref[c].reshape(held, width),
            (((1,), (1,)), ((), ())),
            preferred_element_type=F32,
        )
        for step in range(parts):
            owner = lax.rem(me + step, parts)
            outs[step][c] = sums[c, pl.ds(owner * share, share), :]


def scores_of(feat, holds, parts):
    ckpts, examples, width = feat.shape
    groups = len(holds)
    members, block = holds[0].shape[1:3]
    peers = groups * members
    lanes = (peers * block // LANES + 1) * LANES
    vmem = pl.BlockSpec(memory_space=pltpu.VMEM)
    anywhere = pl.BlockSpec(memory_space=pl.ANY)
    return pl.pallas_call(
        functools.partial(score_kernel, groups=groups, parts=parts),
        out_shape=[jax.ShapeDtypeStruct((ckpts, examples // parts, lanes), F32)] * parts,
        in_specs=[anywhere] * (1 + groups),
        out_specs=[vmem] * parts,
        scratch_shapes=[
            pltpu.VMEM(feat.shape, BF16),
            pltpu.VMEM((ckpts, peers, block, width), BF16),
            pltpu.VMEM((ckpts, examples, lanes), F32),
            pltpu.SemaphoreType.DMA((groups, members)),
            pltpu.SemaphoreType.DMA,
        ],
        compiler_params=pltpu.CompilerParams(vmem_limit_bytes=12 << 20),
        name="scores",
    )(feat, *holds)


def finish_kernel(*refs):
    weight_ref, pieces, out_ref = refs[0], refs[1:-1], refs[-1]
    held = out_ref.shape[1]
    result = jnp.zeros(out_ref.shape, F32)
    for c in range(pieces[0].shape[0]):
        total = pieces[0][c]
        for piece in pieces[1:]:
            total = total + piece[c]
        scale = weight_ref[c] * lax.rsqrt(total[:, held : held + 1] + 1e-06)
        result = result + total[:, :held] * scale
    out_ref[...] = result


def solution(mesh):
    parts = mesh.shape["layer"]
    peers = mesh.shape["dp"]

    def local(grad, act, var, hold, lengths, mask, seed, weight):
        ckpts, _, examples, slots, width = grad.shape
        rank = act.shape[-1]
        cols = hold.shape[-1] // rank
        members = 2 if peers % 2 == 0 else 1
        groups = peers // members
        gathered = [hold[:, 0]]
        for turn in range(1, members):
            ring = [
                (i, i // members * members + (i + members - turn) % members) for i in range(peers)
            ]
            gathered.append(lax.ppermute(hold[:, 0], "dp", ring))
        own = jnp.stack(gathered, axis=1)
        holds = [own]
        for step in range(1, groups):
            ring = [(i, (i + step * members) % peers) for i in range(peers)]
            holds.append(lax.ppermute(own, "dp", ring))
        feat = features_of(
            seed,
            lengths,
            mask.T,
            act.reshape(ckpts, examples * slots, rank),
            grad.reshape(ckpts, examples * slots, width),
            var[:, 0],
            cols,
        )
        pieces = list(scores_of(feat, holds, parts))
        for step in range(1, parts):
            ring = [(i, (i + step) % parts) for i in range(parts)]
            pieces[step] = lax.ppermute(pieces[step], "layer", ring)
        vmem = pl.BlockSpec(memory_space=pltpu.VMEM)
        return pl.pallas_call(
            finish_kernel,
            out_shape=jax.ShapeDtypeStruct((examples // parts, peers * hold.shape[2]), F32),
            in_specs=[pl.BlockSpec(memory_space=pltpu.SMEM)] + [vmem] * parts,
            out_specs=vmem,
            compiler_params=pltpu.CompilerParams(vmem_limit_bytes=12 << 20),
            name="finish",
        )(weight, *pieces)

    placed = (
        P(None, "layer", "dp", None, None),
        P(None, "layer", "dp", None, None),
        P(None, "layer", None, None),
        P(None, "layer", "dp", None),
        P("dp"),
        P("dp", None),
        P(),
        P(),
    )
    return jax.shard_map(
        local, mesh=mesh, in_specs=placed, out_specs=P(("dp", "layer"), None), check_vma=False
    )
```

```python
import functools
import math

import jax
import jax.numpy as jnp
from jax import lax
from jax.experimental import pallas as pl
from jax.experimental.pallas import tpu as pltpu
from jax.sharding import PartitionSpec as P

F32 = jnp.float32
BF16 = jnp.bfloat16
TILE = 256
LANES = 128
AHEAD = 2
READY = 2


def target(index, step, size):
    return index ^ step if size & (size - 1) == 0 else (index + step) % size


def source(index, step, size):
    return index ^ step if size & (size - 1) == 0 else (index + size - step) % size


def feature_kernel(
    seed_ref,
    act_ref,
    grad_hbm,
    var_hbm,
    out_ref,
    grad_raw,
    var_raw,
    lhs_ring,
    scale_ring,
    sign_ring,
    act_blocks,
    feat_buf,
    grad_sems,
    var_sems,
    *,
    ckpts,
    examples,
    slots,
    width,
    cols,
    tiles,
):
    chunk = tiles * TILE
    chunks = width // chunk
    total = ckpts * chunks
    pairs = examples // 2
    per_unit = pairs // 2
    sign_rows = sign_ring.shape[0]
    inv_root = 1.0 / math.sqrt(width)

    def copies(it):
        c, q = it // chunks, it % chunks
        at = pl.ds(pl.multiple_of(q * chunk, chunk), chunk)
        return (
            pltpu.make_async_copy(grad_hbm.at[c, :, at], grad_raw.at[c, :, at], grad_sems.at[it]),
            pltpu.make_async_copy(var_hbm.at[c, at, :], var_raw.at[c, at, :], var_sems.at[it]),
        )


    for copy in (*copies(0), *copies(1)):
        copy.start()
    act_blocks[...] = jnp.zeros_like(act_blocks)
    hash_base = (
        lax.axis_index("layer") * jnp.int32(668265263) + seed_ref[0] * jnp.int32(374761393)
    )
    for pair in range(pairs):
        for c in range(ckpts):
            at = 2 * pair * slots
            first = act_ref[c, at : at + slots, :].astype(F32)
            second = act_ref[c, at + slots : at + 2 * slots, :].astype(F32)
            blank = jnp.zeros_like(first)
            act_blocks[c * pairs + pair, at : at + 2 * slots, :] = jnp.concatenate(
                [jnp.concatenate([first, blank], 1), jnp.concatenate([blank, second], 1)], 0
            ).astype(BF16)

    def prepare(it, t, part):
        c, q = it // chunks, it % chunks
        base = q * chunk + t * TILE
        here = t * TILE
        if part < 2:
            half = part * LANES
            src = grad_raw[c, :, pl.ds(pl.multiple_of(base + half, LANES), LANES)]
            lhs_ring[here + half : here + half + LANES, :] = jnp.transpose(src)
        elif part == 2:
            moment = var_raw[c, pl.ds(pl.multiple_of(base, TILE), TILE), :].astype(F32)
            scale_ring[here : here + TILE, :] = 1.0 / (jnp.sqrt(moment) + 1e-08)
        else:
            d = lax.broadcasted_iota(jnp.int32, (sign_rows, TILE), 1) + base
            k = lax.broadcasted_iota(jnp.int32, (sign_rows, TILE), 0)
            m = d * jnp.int32(1103515245) + k * jnp.int32(12345) + hash_base
            m = m ^ (m >> 15)
            m = m * jnp.int32(747796405)
            m = m ^ (m >> 13)
            sign = (2 * ((m >> 7) & 1) - 1).astype(F32)
            sign_ring[:, here : here + TILE] = jnp.where(k < cols, sign, 0.0).astype(BF16)

    for copy in copies(0):
        copy.wait()
    for it in range(2, total):
        for copy in copies(it):
            copy.start()
    for t in range(READY):
        for part in range(4):
            prepare(0, t, part)

    def scoped(*accs):
        depth = AHEAD + 1
        outer_acc = [accs[m * depth : (m + 1) * depth] for m in (0, 1)]
        proj_acc = [accs[2 * depth + m * per_unit : 2 * depth + (m + 1) * per_unit] for m in (0, 1)]
        steps = [(t, j) for t in range(tiles) for j in range(per_unit)]

        def outer(c, m, n):
            t, j = steps[n]
            tokens = lhs_ring[t * TILE : (t + 1) * TILE, :]
            pltpu.matmul_push_rhs(act_blocks[c * pairs + m * per_unit + j], 0, m)
            pltpu.matmul_acc_lhs(
                outer_acc[m][n % depth], jnp.concatenate([tokens, tokens], 1), load_staged_rhs=0
            )

        def project(m, n):
            t, j = steps[n]
            at = slice(t * TILE, (t + 1) * TILE)
            summed = pltpu.matmul_pop(outer_acc[m][n % depth])
            scale = scale_ring[at, :]
            scaled = (summed * jnp.concatenate([scale, scale], 1)).astype(BF16)
            pltpu.matmul_push_rhs(scaled, 1, m)
            pltpu.matmul_acc_lhs(proj_acc[m][j], sign_ring[:, at], load_staged_rhs=1)

        def one_chunk(c, q):
            it = c * chunks + q
            following = jnp.minimum(it + 1, total - 1)

            @pl.when(it + 1 < total)
            def _():
                for copy in copies(it + 1):
                    copy.wait()

            for n in range(1, AHEAD):
                for m in (0, 1):
                    outer(c, m, n)
            for n in range(len(steps)):
                for m in (0, 1):
                    if n + AHEAD < len(steps):
                        outer(c, m, n + AHEAD)
                    project(m, n)
                    if n == len(steps) - 2:
                        outer(following // chunks, m, 0)
                t, j = steps[n]
                for part in range(j * 4 // per_unit, (j + 1) * 4 // per_unit):
                    if t + READY < tiles:
                        prepare(it, t + READY, part)
                    else:
                        prepare(following, t + READY - tiles, part)

        def one_ckpt(c, carry):
            def body(q, inner):
                one_chunk(c, q)
                return inner

            lax.fori_loop(0, chunks, body, 0)
            for m in (0, 1):
                for j in range(per_unit):
                    total_sum = pltpu.matmul_pop(proj_acc[m][j])
                    for half in range(2):
                        e = 2 * (m * per_unit + j) + half
                        feat_buf[e] = total_sum[:cols, half * LANES : (half + 1) * LANES] * inv_root
            for k in range(cols):
                out_ref[c, :, k * LANES : (k + 1) * LANES] = feat_buf[:, k, :].astype(BF16)
            return carry

        for m in (0, 1):
            outer(0, m, 0)
        lax.fori_loop(0, ckpts, one_ckpt, 0)
        for m in (0, 1):
            pltpu.matmul_pop(outer_acc[m][0])

    pl.run_scoped(
        scoped,
        *[pltpu.ACC(m)((TILE, TILE), F32) for m in (0, 1) for _ in range(AHEAD + 1)],
        *[pltpu.ACC(m)((sign_rows, TILE), F32) for m in (0, 1) for _ in range(per_unit)],
    )


def features_of(seed, act, grad, var, slots, cols):
    ckpts, rows, width = grad.shape
    examples = rows // slots
    tiles = 8
    chunk = tiles * TILE
    pairs = examples // 2
    sign_rows = -(-cols // 16) * 16
    vmem = pl.BlockSpec(memory_space=pltpu.VMEM)
    hbm = pl.BlockSpec(memory_space=pltpu.HBM)
    kernel = functools.partial(
        feature_kernel,
        ckpts=ckpts,
        examples=examples,
        slots=slots,
        width=width,
        cols=cols,
        tiles=tiles,
    )
    return pl.pallas_call(
        kernel,
        out_shape=jax.ShapeDtypeStruct((ckpts, examples, cols * LANES), BF16),
        in_specs=[pl.BlockSpec(memory_space=pltpu.SMEM), vmem, hbm, hbm],
        out_specs=vmem,
        scratch_shapes=[
            pltpu.VMEM((ckpts, rows, width), BF16),
            pltpu.VMEM((ckpts, width, LANES), BF16),
            pltpu.VMEM((chunk, LANES), BF16),
            pltpu.VMEM((chunk, LANES), F32),
            pltpu.VMEM((sign_rows, chunk), BF16),
            pltpu.VMEM((ckpts * pairs, TILE, TILE), BF16),
            pltpu.VMEM((examples, cols, LANES), F32),
            pltpu.SemaphoreType.DMA((ckpts * width // chunk,)),
            pltpu.SemaphoreType.DMA((ckpts * width // chunk,)),
        ],
        compiler_params=pltpu.CompilerParams(vmem_limit_bytes=53 << 20),
        cost_estimate=pl.CostEstimate(
            flops=40_000_000_000, bytes_accessed=9_000_000, transcendentals=0
        ),
        name="features",
    )(seed, act, grad, var)


def score_kernel(*refs, groups, parts):
    weight_ref, feat_ref, holds = refs[0], refs[1], refs[2 : 2 + groups]
    outs, (turned, sums) = refs[2 + groups : 2 + groups + parts], refs[2 + groups + parts :]
    ckpts, examples, width = feat_ref.shape
    members, block = holds[0].shape[1:3]
    held = groups * members * block
    share = examples // parts
    mine = lax.axis_index("dp")
    me = lax.axis_index("layer")
    group, member = mine // members, lax.rem(mine, members)
    for c in range(ckpts):
        feat = feat_ref[c]
        stack = jnp.concatenate([hold[c].reshape(members * block, width) for hold in holds], 0)
        found = lax.dot_general(
            stack, feat, (((1,), (1,)), ((), ())), preferred_element_type=F32
        )
        for step in range(groups):
            first = source(group, step, groups) * members
            for turn in range(members):
                index = first + lax.rem(member + turn, members)
                at = (step * members + turn) * block
                turned[c, pl.ds(pl.multiple_of(index * block, block), block), :] = found[
                    at : at + block
                ]
        wide = feat.astype(F32)
        norm = jnp.sum(wide * wide, axis=1, keepdims=True)
        sums[c, :, :held] = jnp.transpose(turned[c]) * weight_ref[c]
        sums[c, :, held:] = jnp.broadcast_to(norm, (examples, sums.shape[2] - held))
        for step in range(parts):
            owner = lax.rem(me + step, parts)
            outs[step][c] = sums[c, pl.ds(owner * share, share), :]


def scores_of(weight, feat, holds, parts):
    ckpts, examples, width = feat.shape
    groups = len(holds)
    members, block = holds[0].shape[1:3]
    held = groups * members * block
    lanes = (held // LANES + 1) * LANES
    vmem = pl.BlockSpec(memory_space=pltpu.VMEM)
    return pl.pallas_call(
        functools.partial(score_kernel, groups=groups, parts=parts),
        out_shape=[jax.ShapeDtypeStruct((ckpts, examples // parts, lanes), F32)] * parts,
        in_specs=[pl.BlockSpec(memory_space=pltpu.SMEM)] + [vmem] * (1 + groups),
        out_specs=[vmem] * parts,
        scratch_shapes=[
            pltpu.VMEM((ckpts, held, examples), F32),
            pltpu.VMEM((ckpts, examples, lanes), F32),
        ],
        compiler_params=pltpu.CompilerParams(vmem_limit_bytes=12 << 20),
        name="scores",
    )(weight, feat, *holds)


def finish_kernel(*refs):
    pieces, out_ref = refs[:-1], refs[-1]
    held = out_ref.shape[1]
    result = jnp.zeros(out_ref.shape, F32)
    for c in range(pieces[0].shape[0]):
        total = pieces[0][c]
        for piece in pieces[1:]:
            total = total + piece[c]
        result = result + total[:, :held] * lax.rsqrt(total[:, held : held + 1] + 1e-06)
    out_ref[...] = result


def solution(mesh):
    parts = mesh.shape["layer"]
    peers = mesh.shape["dp"]

    def local(grad, act, var, hold, lengths, mask, seed, weight):
        ckpts, _, examples, slots, width = grad.shape
        rank = act.shape[-1]
        cols = hold.shape[-1] // rank
        members = 2 if peers % 2 == 0 else 1
        groups = peers // members
        gathered = [hold[:, 0]]
        for turn in range(1, members):
            ring = [
                (i, i // members * members + (i + members - turn) % members) for i in range(peers)
            ]
            gathered.append(lax.ppermute(hold[:, 0], "dp", ring))
        own = jnp.stack(gathered, axis=1)
        holds = [own]
        for step in range(1, groups):
            ring = [
                (i, target(i // members, step, groups) * members + i % members) for i in range(peers)
            ]
            holds.append(lax.ppermute(own, "dp", ring))
        valid = (mask == 1) & (jnp.arange(slots, dtype=jnp.int32) < lengths[:, None])
        valid = valid[None, :, :, None]
        feat = features_of(
            seed,
            jnp.where(valid, act[:, 0], 0).reshape(ckpts, examples * slots, rank),
            grad.reshape(ckpts, examples * slots, width),
            var[:, 0],
            slots,
            cols,
        )
        pieces = list(scores_of(weight, feat, holds, parts))
        for step in range(1, parts):
            ring = [(i, (i + step) % parts) for i in range(parts)]
            pieces[step] = lax.ppermute(pieces[step], "layer", ring)
        vmem = pl.BlockSpec(memory_space=pltpu.VMEM)
        return pl.pallas_call(
            finish_kernel,
            out_shape=jax.ShapeDtypeStruct((examples // parts, peers * hold.shape[2]), F32),
            in_specs=[vmem] * parts,
            out_specs=vmem,
            compiler_params=pltpu.CompilerParams(vmem_limit_bytes=12 << 20),
            name="finish",
        )(*pieces)

    placed = (
        P(None, "layer", "dp", None, None),
        P(None, "layer", "dp", None, None),
        P(None, "layer", None, None),
        P(None, "layer", "dp", None),
        P("dp"),
        P("dp", None),
        P(),
        P(),
    )
    return jax.shard_map(
        local, mesh=mesh, in_specs=placed, out_specs=P(("dp", "layer"), None), check_vma=False
    )
```

```python
import functools
import math

import jax
import jax.numpy as jnp
from jax import lax
from jax.experimental import pallas as pl
from jax.experimental.pallas import tpu as pltpu
from jax.sharding import PartitionSpec as P

F32 = jnp.float32
BF16 = jnp.bfloat16
TILE = 256
LANES = 128
AHEAD = 2
READY = 2


def target(index, step, size):
    return index ^ step if size & (size - 1) == 0 else (index + step) % size


def source(index, step, size):
    return index ^ step if size & (size - 1) == 0 else (index + size - step) % size


def feature_kernel(
    seed_ref,
    len_hbm,
    mask_hbm,
    act_hbm,
    grad_hbm,
    var_hbm,
    out_ref,
    len_ref,
    mask_ref,
    act_ref,
    grad_raw,
    var_raw,
    lhs_ring,
    scale_ring,
    sign_ring,
    act_blocks,
    feat_buf,
    small_sems,
    grad_sems,
    var_sems,
    *,
    ckpts,
    examples,
    slots,
    width,
    cols,
    tiles,
):
    chunk = tiles * TILE
    chunks = width // chunk
    total = ckpts * chunks
    pairs = examples // 2
    per_unit = pairs // 2
    sign_rows = sign_ring.shape[0]
    inv_root = 1.0 / math.sqrt(width)

    def copies(it):
        c, q = it // chunks, it % chunks
        at = pl.ds(pl.multiple_of(q * chunk, chunk), chunk)
        return (
            pltpu.make_async_copy(grad_hbm.at[c, :, at], grad_raw.at[c, :, at], grad_sems.at[it]),
            pltpu.make_async_copy(var_hbm.at[c, at, :], var_raw.at[c, at, :], var_sems.at[it]),
        )


    small = [
        pltpu.make_async_copy(src, dst, small_sems.at[i])
        for i, (src, dst) in enumerate(
            ((len_hbm, len_ref), (mask_hbm, mask_ref), (act_hbm, act_ref))
        )
    ]
    for copy in (*small, *copies(0), *copies(1)):
        copy.start()
    act_blocks[...] = jnp.zeros_like(act_blocks)
    for copy in small:
        copy.wait()
    hash_base = (
        lax.axis_index("layer") * jnp.int32(668265263) + seed_ref[0] * jnp.int32(374761393)
    )
    slot_ids = lax.broadcasted_iota(jnp.int32, (slots, 1), 0)
    for pair in range(pairs):
        marks = [
            (mask_ref[:, e : e + 1] == 1) & (slot_ids < len_ref[e])
            for e in (2 * pair, 2 * pair + 1)
        ]
        for c in range(ckpts):
            at = 2 * pair * slots
            first = jnp.where(marks[0], act_ref[c, at : at + slots, :].astype(F32), 0.0)
            second = jnp.where(marks[1], act_ref[c, at + slots : at + 2 * slots, :].astype(F32), 0.0)
            blank = jnp.zeros_like(first)
            act_blocks[c * pairs + pair, at : at + 2 * slots, :] = jnp.concatenate(
                [jnp.concatenate([first, blank], 1), jnp.concatenate([blank, second], 1)], 0
            ).astype(BF16)

    def prepare(it, t, part):
        c, q = it // chunks, it % chunks
        base = q * chunk + t * TILE
        here = t * TILE
        if part < 2:
            half = part * LANES
            src = grad_raw[c, :, pl.ds(pl.multiple_of(base + half, LANES), LANES)]
            lhs_ring[here + half : here + half + LANES, :] = jnp.transpose(src)
        elif part == 2:
            moment = var_raw[c, pl.ds(pl.multiple_of(base, TILE), TILE), :].astype(F32)
            scale_ring[here : here + TILE, :] = 1.0 / (jnp.sqrt(moment) + 1e-08)
        else:
            d = lax.broadcasted_iota(jnp.int32, (sign_rows, TILE), 1) + base
            k = lax.broadcasted_iota(jnp.int32, (sign_rows, TILE), 0)
            m = d * jnp.int32(1103515245) + k * jnp.int32(12345) + hash_base
            m = m ^ (m >> 15)
            m = m * jnp.int32(747796405)
            m = m ^ (m >> 13)
            sign = (2 * ((m >> 7) & 1) - 1).astype(F32)
            sign_ring[:, here : here + TILE] = jnp.where(k < cols, sign, 0.0).astype(BF16)

    for copy in copies(0):
        copy.wait()
    for it in range(2, total):
        for copy in copies(it):
            copy.start()
    for t in range(READY):
        for part in range(4):
            prepare(0, t, part)

    def scoped(*accs):
        depth = AHEAD + 1
        outer_acc = [accs[m * depth : (m + 1) * depth] for m in (0, 1)]
        proj_acc = [accs[2 * depth + m * per_unit : 2 * depth + (m + 1) * per_unit] for m in (0, 1)]
        steps = [(t, j) for t in range(tiles) for j in range(per_unit)]

        def outer(c, m, n):
            t, j = steps[n]
            tokens = lhs_ring[t * TILE : (t + 1) * TILE, :]
            pltpu.matmul_push_rhs(act_blocks[c * pairs + m * per_unit + j], 0, m)
            pltpu.matmul_acc_lhs(
                outer_acc[m][n % depth], jnp.concatenate([tokens, tokens], 1), load_staged_rhs=0
            )

        def project(m, n):
            t, j = steps[n]
            at = slice(t * TILE, (t + 1) * TILE)
            summed = pltpu.matmul_pop(outer_acc[m][n % depth])
            scale = scale_ring[at, :]
            scaled = (summed * jnp.concatenate([scale, scale], 1)).astype(BF16)
            pltpu.matmul_push_rhs(scaled, 1, m)
            pltpu.matmul_acc_lhs(proj_acc[m][j], sign_ring[:, at], load_staged_rhs=1)

        def one_chunk(c, q):
            it = c * chunks + q
            following = jnp.minimum(it + 1, total - 1)

            @pl.when(it + 1 < total)
            def _():
                for copy in copies(it + 1):
                    copy.wait()

            for n in range(1, AHEAD):
                for m in (0, 1):
                    outer(c, m, n)
            for n in range(len(steps)):
                for m in (0, 1):
                    if n + AHEAD < len(steps):
                        outer(c, m, n + AHEAD)
                    project(m, n)
                    if n == len(steps) - 2:
                        outer(following // chunks, m, 0)
                t, j = steps[n]
                for part in range(j * 4 // per_unit, (j + 1) * 4 // per_unit):
                    if t + READY < tiles:
                        prepare(it, t + READY, part)
                    else:
                        prepare(following, t + READY - tiles, part)

        def one_ckpt(c, carry):
            def body(q, inner):
                one_chunk(c, q)
                return inner

            lax.fori_loop(0, chunks, body, 0)
            for m in (0, 1):
                for j in range(per_unit):
                    total_sum = pltpu.matmul_pop(proj_acc[m][j])
                    for half in range(2):
                        e = 2 * (m * per_unit + j) + half
                        feat_buf[e] = total_sum[:cols, half * LANES : (half + 1) * LANES] * inv_root
            for k in range(cols):
                out_ref[c, :, k * LANES : (k + 1) * LANES] = feat_buf[:, k, :].astype(BF16)
            return carry

        for m in (0, 1):
            outer(0, m, 0)
        lax.fori_loop(0, ckpts, one_ckpt, 0)
        for m in (0, 1):
            pltpu.matmul_pop(outer_acc[m][0])

    pl.run_scoped(
        scoped,
        *[pltpu.ACC(m)((TILE, TILE), F32) for m in (0, 1) for _ in range(AHEAD + 1)],
        *[pltpu.ACC(m)((sign_rows, TILE), F32) for m in (0, 1) for _ in range(per_unit)],
    )


def features_of(seed, lengths, mask, act, grad, var, cols):
    ckpts, rows, width = grad.shape
    slots, examples = mask.shape
    stay = [
        pltpu.with_memory_space_constraint(x, pltpu.HBM) for x in (lengths, mask, act, grad, var)
    ]
    tiles = 8
    chunk = tiles * TILE
    pairs = examples // 2
    sign_rows = -(-cols // 16) * 16
    vmem = pl.BlockSpec(memory_space=pltpu.VMEM)
    hbm = pl.BlockSpec(memory_space=pltpu.HBM)
    kernel = functools.partial(
        feature_kernel,
        ckpts=ckpts,
        examples=examples,
        slots=slots,
        width=width,
        cols=cols,
        tiles=tiles,
    )
    return pl.pallas_call(
        kernel,
        out_shape=jax.ShapeDtypeStruct((ckpts, examples, cols * LANES), BF16),
        in_specs=[pl.BlockSpec(memory_space=pltpu.SMEM)] + [hbm] * 5,
        out_specs=vmem,
        scratch_shapes=[
            pltpu.SMEM(lengths.shape, jnp.int32),
            pltpu.VMEM(mask.shape, jnp.int32),
            pltpu.VMEM(act.shape, BF16),
            pltpu.VMEM((ckpts, rows, width), BF16),
            pltpu.VMEM((ckpts, width, LANES), BF16),
            pltpu.VMEM((chunk, LANES), BF16),
            pltpu.VMEM((chunk, LANES), F32),
            pltpu.VMEM((sign_rows, chunk), BF16),
            pltpu.VMEM((ckpts * pairs, TILE, TILE), BF16),
            pltpu.VMEM((examples, cols, LANES), F32),
            pltpu.SemaphoreType.DMA((3,)),
            pltpu.SemaphoreType.DMA((ckpts * width // chunk,)),
            pltpu.SemaphoreType.DMA((ckpts * width // chunk,)),
        ],
        compiler_params=pltpu.CompilerParams(vmem_limit_bytes=40 << 20),
        cost_estimate=pl.CostEstimate(
            flops=40_000_000_000, bytes_accessed=9_000_000, transcendentals=0
        ),
        name="features",
    )(seed, *stay)


def score_kernel(*refs, groups, parts):
    weight_ref, feat_ref, holds = refs[0], refs[1], refs[2 : 2 + groups]
    outs, (turned, sums) = refs[2 + groups : 2 + groups + parts], refs[2 + groups + parts :]
    ckpts, examples, width = feat_ref.shape
    members, block = holds[0].shape[1:3]
    held = groups * members * block
    share = examples // parts
    mine = lax.axis_index("dp")
    me = lax.axis_index("layer")
    group, member = mine // members, lax.rem(mine, members)
    for c in range(ckpts):
        feat = feat_ref[c]
        stack = jnp.concatenate([hold[c].reshape(members * block, width) for hold in holds], 0)
        found = lax.dot_general(
            stack, feat, (((1,), (1,)), ((), ())), preferred_element_type=F32
        )
        for step in range(groups):
            first = source(group, step, groups) * members
            for turn in range(members):
                index = first + lax.rem(member + turn, members)
                at = (step * members + turn) * block
                turned[c, pl.ds(pl.multiple_of(index * block, block), block), :] = found[
                    at : at + block
                ]
        wide = feat.astype(F32)
        norm = jnp.sum(wide * wide, axis=1, keepdims=True)
        sums[c, :, :held] = jnp.transpose(turned[c]) * weight_ref[c]
        sums[c, :, held:] = jnp.broadcast_to(norm, (examples, sums.shape[2] - held))
        for step in range(parts):
            owner = lax.rem(me + step, parts)
            outs[step][c] = sums[c, pl.ds(owner * share, share), :]


def scores_of(weight, feat, holds, parts):
    ckpts, examples, width = feat.shape
    groups = len(holds)
    members, block = holds[0].shape[1:3]
    held = groups * members * block
    lanes = (held // LANES + 1) * LANES
    vmem = pl.BlockSpec(memory_space=pltpu.VMEM)
    return pl.pallas_call(
        functools.partial(score_kernel, groups=groups, parts=parts),
        out_shape=[jax.ShapeDtypeStruct((ckpts, examples // parts, lanes), F32)] * parts,
        in_specs=[pl.BlockSpec(memory_space=pltpu.SMEM)] + [vmem] * (1 + groups),
        out_specs=[vmem] * parts,
        scratch_shapes=[
            pltpu.VMEM((ckpts, held, examples), F32),
            pltpu.VMEM((ckpts, examples, lanes), F32),
        ],
        compiler_params=pltpu.CompilerParams(vmem_limit_bytes=12 << 20),
        name="scores",
    )(weight, feat, *holds)


def finish_kernel(*refs):
    pieces, out_ref = refs[:-1], refs[-1]
    held = out_ref.shape[1]
    result = jnp.zeros(out_ref.shape, F32)
    for c in range(pieces[0].shape[0]):
        total = pieces[0][c]
        for piece in pieces[1:]:
            total = total + piece[c]
        result = result + total[:, :held] * lax.rsqrt(total[:, held : held + 1] + 1e-06)
    out_ref[...] = result


def place_kernel(*refs, turn):
    block_ref, out_ref, sem = refs[0], refs[-2], refs[-1]
    copy = pltpu.make_async_copy(block_ref, out_ref.at[:, turn], sem)
    copy.start()
    copy.wait()


def together(blocks):
    ckpts, *rest = blocks[0].shape
    anywhere = pl.BlockSpec(memory_space=pl.ANY)
    joined = ()
    for turn, block in enumerate(blocks):
        if turn == 0:
            block = pltpu.with_memory_space_constraint(block, pltpu.HBM)
        joined = (
            pl.pallas_call(
                functools.partial(place_kernel, turn=turn),
                out_shape=jax.ShapeDtypeStruct((ckpts, len(blocks), *rest), block.dtype),
                in_specs=[anywhere] * (1 + len(joined)),
                out_specs=anywhere,
                scratch_shapes=[pltpu.SemaphoreType.DMA],
                input_output_aliases={1: 0} if joined else {},
                compiler_params=pltpu.CompilerParams(vmem_limit_bytes=12 << 20),
                name=f"place{turn}",
            )(block, *joined),
        )
    return joined[0]


def solution(mesh):
    parts = mesh.shape["layer"]
    peers = mesh.shape["dp"]

    def local(grad, act, var, hold, lengths, mask, seed, weight):
        ckpts, _, examples, slots, width = grad.shape
        rank = act.shape[-1]
        cols = hold.shape[-1] // rank
        members = 2 if peers % 2 == 0 else 1
        groups = peers // members
        gathered = [hold[:, 0]]
        for turn in range(1, members):
            ring = [
                (i, i // members * members + (i + members - turn) % members) for i in range(peers)
            ]
            gathered.append(lax.ppermute(hold[:, 0], "dp", ring))
        own = together(gathered)
        holds = [own]
        for step in range(1, groups):
            ring = [
                (i, target(i // members, step, groups) * members + i % members) for i in range(peers)
            ]
            holds.append(lax.ppermute(own, "dp", ring))
        feat = features_of(
            seed,
            lengths,
            mask.T,
            act.reshape(ckpts, examples * slots, rank),
            grad.reshape(ckpts, examples * slots, width),
            var[:, 0],
            cols,
        )
        pieces = list(scores_of(weight, feat, holds, parts))
        for step in range(1, parts):
            ring = [(i, (i + step) % parts) for i in range(parts)]
            pieces[step] = lax.ppermute(pieces[step], "layer", ring)
        vmem = pl.BlockSpec(memory_space=pltpu.VMEM)
        return pl.pallas_call(
            finish_kernel,
            out_shape=jax.ShapeDtypeStruct((examples // parts, peers * hold.shape[2]), F32),
            in_specs=[vmem] * parts,
            out_specs=vmem,
            compiler_params=pltpu.CompilerParams(vmem_limit_bytes=12 << 20),
            name="finish",
        )(*pieces)

    placed = (
        P(None, "layer", "dp", None, None),
        P(None, "layer", "dp", None, None),
        P(None, "layer", None, None),
        P(None, "layer", "dp", None),
        P("dp"),
        P("dp", None),
        P(),
        P(),
    )
    return jax.shard_map(
        local, mesh=mesh, in_specs=placed, out_specs=P(("dp", "layer"), None), check_vma=False
    )
```

```python
import functools
import math

import jax
import jax.numpy as jnp
from jax import lax
from jax.experimental import pallas as pl
from jax.experimental.pallas import tpu as pltpu
from jax.sharding import PartitionSpec as P

F32 = jnp.float32
BF16 = jnp.bfloat16
TILE = 256
LANES = 128
AHEAD = 2
READY = 2


def target(index, step, size):
    return index ^ step if size & (size - 1) == 0 else (index + step) % size


def source(index, step, size):
    return index ^ step if size & (size - 1) == 0 else (index + size - step) % size


def feature_kernel(
    seed_ref,
    len_ref,
    mask_ref,
    act_ref,
    grad_raw,
    var_raw,
    out_ref,
    lhs_ring,
    scale_ring,
    sign_ring,
    act_blocks,
    feat_buf,
    *,
    ckpts,
    examples,
    slots,
    width,
    cols,
    tiles,
):
    chunk = tiles * TILE
    chunks = width // chunk
    total = ckpts * chunks
    pairs = examples // 2
    per_unit = pairs // 2
    sign_rows = sign_ring.shape[0]
    inv_root = 1.0 / math.sqrt(width)

    act_blocks[...] = jnp.zeros_like(act_blocks)
    hash_base = (
        lax.axis_index("layer") * jnp.int32(668265263) + seed_ref[0] * jnp.int32(374761393)
    )
    slot_ids = lax.broadcasted_iota(jnp.int32, (slots, 1), 0)
    for pair in range(pairs):
        marks = [
            (mask_ref[:, e : e + 1] == 1) & (slot_ids < len_ref[e])
            for e in (2 * pair, 2 * pair + 1)
        ]
        for c in range(ckpts):
            at = 2 * pair * slots
            first = jnp.where(marks[0], act_ref[c, at : at + slots, :].astype(F32), 0.0)
            second = jnp.where(marks[1], act_ref[c, at + slots : at + 2 * slots, :].astype(F32), 0.0)
            blank = jnp.zeros_like(first)
            act_blocks[c * pairs + pair, at : at + 2 * slots, :] = jnp.concatenate(
                [jnp.concatenate([first, blank], 1), jnp.concatenate([blank, second], 1)], 0
            ).astype(BF16)

    def prepare(it, t, part):
        c, q = it // chunks, it % chunks
        base = q * chunk + t * TILE
        here = t * TILE
        if part < 2:
            half = part * LANES
            src = grad_raw[c, :, pl.ds(pl.multiple_of(base + half, LANES), LANES)]
            lhs_ring[here + half : here + half + LANES, :] = jnp.transpose(src)
        elif part == 2:
            moment = var_raw[c, pl.ds(pl.multiple_of(base, TILE), TILE), :].astype(F32)
            scale_ring[here : here + TILE, :] = 1.0 / (jnp.sqrt(moment) + 1e-08)
        else:
            d = lax.broadcasted_iota(jnp.int32, (sign_rows, TILE), 1) + base
            k = lax.broadcasted_iota(jnp.int32, (sign_rows, TILE), 0)
            m = d * jnp.int32(1103515245) + k * jnp.int32(12345) + hash_base
            m = m ^ (m >> 15)
            m = m * jnp.int32(747796405)
            m = m ^ (m >> 13)
            sign = (2 * ((m >> 7) & 1) - 1).astype(F32)
            sign_ring[:, here : here + TILE] = jnp.where(k < cols, sign, 0.0).astype(BF16)

    for t in range(READY):
        for part in range(4):
            prepare(0, t, part)

    def scoped(*accs):
        depth = AHEAD + 1
        outer_acc = [accs[m * depth : (m + 1) * depth] for m in (0, 1)]
        proj_acc = [accs[2 * depth + m * per_unit : 2 * depth + (m + 1) * per_unit] for m in (0, 1)]
        steps = [(t, j) for t in range(tiles) for j in range(per_unit)]

        def outer(c, m, n):
            t, j = steps[n]
            tokens = lhs_ring[t * TILE : (t + 1) * TILE, :]
            pltpu.matmul_push_rhs(act_blocks[c * pairs + m * per_unit + j], 0, m)
            pltpu.matmul_acc_lhs(
                outer_acc[m][n % depth], jnp.concatenate([tokens, tokens], 1), load_staged_rhs=0
            )

        def project(m, n):
            t, j = steps[n]
            at = slice(t * TILE, (t + 1) * TILE)
            summed = pltpu.matmul_pop(outer_acc[m][n % depth])
            scale = scale_ring[at, :]
            scaled = (summed * jnp.concatenate([scale, scale], 1)).astype(BF16)
            pltpu.matmul_push_rhs(scaled, 1, m)
            pltpu.matmul_acc_lhs(proj_acc[m][j], sign_ring[:, at], load_staged_rhs=1)

        def one_chunk(c, q):
            it = c * chunks + q
            following = jnp.minimum(it + 1, total - 1)

            for n in range(1, AHEAD):
                for m in (0, 1):
                    outer(c, m, n)
            for n in range(len(steps)):
                for m in (0, 1):
                    if n + AHEAD < len(steps):
                        outer(c, m, n + AHEAD)
                    project(m, n)
                    if n == len(steps) - 2:
                        outer(following // chunks, m, 0)
                t, j = steps[n]
                for part in range(j * 4 // per_unit, (j + 1) * 4 // per_unit):
                    if t + READY < tiles:
                        prepare(it, t + READY, part)
                    else:
                        prepare(following, t + READY - tiles, part)

        def one_ckpt(c, carry):
            def body(q, inner):
                one_chunk(c, q)
                return inner

            lax.fori_loop(0, chunks, body, 0)
            for m in (0, 1):
                for j in range(per_unit):
                    total_sum = pltpu.matmul_pop(proj_acc[m][j])
                    for half in range(2):
                        e = 2 * (m * per_unit + j) + half
                        feat_buf[e] = total_sum[:cols, half * LANES : (half + 1) * LANES] * inv_root
            for k in range(cols):
                out_ref[c, :, k * LANES : (k + 1) * LANES] = feat_buf[:, k, :].astype(BF16)
            return carry

        for m in (0, 1):
            outer(0, m, 0)
        lax.fori_loop(0, ckpts, one_ckpt, 0)
        for m in (0, 1):
            pltpu.matmul_pop(outer_acc[m][0])

    pl.run_scoped(
        scoped,
        *[pltpu.ACC(m)((TILE, TILE), F32) for m in (0, 1) for _ in range(AHEAD + 1)],
        *[pltpu.ACC(m)((sign_rows, TILE), F32) for m in (0, 1) for _ in range(per_unit)],
    )


def features_of(seed, lengths, mask, act, grad, var, cols):
    ckpts, rows, width = grad.shape
    slots, examples = mask.shape
    tiles = 8
    chunk = tiles * TILE
    pairs = examples // 2
    sign_rows = -(-cols // 16) * 16
    vmem = pl.BlockSpec(memory_space=pltpu.VMEM)
    smem = pl.BlockSpec(memory_space=pltpu.SMEM)
    kernel = functools.partial(
        feature_kernel,
        ckpts=ckpts,
        examples=examples,
        slots=slots,
        width=width,
        cols=cols,
        tiles=tiles,
    )
    return pl.pallas_call(
        kernel,
        out_shape=jax.ShapeDtypeStruct((ckpts, examples, cols * LANES), BF16),
        in_specs=[smem, smem] + [vmem] * 4,
        out_specs=vmem,
        scratch_shapes=[
            pltpu.VMEM((chunk, LANES), BF16),
            pltpu.VMEM((chunk, LANES), F32),
            pltpu.VMEM((sign_rows, chunk), BF16),
            pltpu.VMEM((ckpts * pairs, TILE, TILE), BF16),
            pltpu.VMEM((examples, cols, LANES), F32),
        ],
        compiler_params=pltpu.CompilerParams(vmem_limit_bytes=24 << 20),
        cost_estimate=pl.CostEstimate(
            flops=40_000_000_000, bytes_accessed=9_000_000, transcendentals=0
        ),
        name="features",
    )(seed, lengths, mask, act, grad, var)


def score_kernel(*refs, groups, parts):
    weight_ref, feat_ref, holds = refs[0], refs[1], refs[2 : 2 + groups]
    outs, (turned, sums) = refs[2 + groups : 2 + groups + parts], refs[2 + groups + parts :]
    ckpts, examples, width = feat_ref.shape
    members, block = holds[0].shape[1:3]
    held = groups * members * block
    share = examples // parts
    mine = lax.axis_index("dp")
    me = lax.axis_index("layer")
    group, member = mine // members, lax.rem(mine, members)
    for c in range(ckpts):
        feat = feat_ref[c]
        stack = jnp.concatenate([hold[c].reshape(members * block, width) for hold in holds], 0)
        found = lax.dot_general(
            stack, feat, (((1,), (1,)), ((), ())), preferred_element_type=F32
        )
        for step in range(groups):
            first = source(group, step, groups) * members
            for turn in range(members):
                index = first + lax.rem(member + turn, members)
                at = (step * members + turn) * block
                turned[c, pl.ds(pl.multiple_of(index * block, block), block), :] = found[
                    at : at + block
                ]
        wide = feat.astype(F32)
        norm = jnp.sum(wide * wide, axis=1, keepdims=True)
        sums[c, :, :held] = jnp.transpose(turned[c]) * weight_ref[c]
        sums[c, :, held:] = jnp.broadcast_to(norm, (examples, sums.shape[2] - held))
        for step in range(parts):
            owner = lax.rem(me + step, parts)
            outs[step][c] = sums[c, pl.ds(owner * share, share), :]


def scores_of(weight, feat, holds, parts):
    ckpts, examples, width = feat.shape
    groups = len(holds)
    members, block = holds[0].shape[1:3]
    held = groups * members * block
    lanes = (held // LANES + 1) * LANES
    vmem = pl.BlockSpec(memory_space=pltpu.VMEM)
    return pl.pallas_call(
        functools.partial(score_kernel, groups=groups, parts=parts),
        out_shape=[jax.ShapeDtypeStruct((ckpts, examples // parts, lanes), F32)] * parts,
        in_specs=[pl.BlockSpec(memory_space=pltpu.SMEM)] + [vmem] * (1 + groups),
        out_specs=[vmem] * parts,
        scratch_shapes=[
            pltpu.VMEM((ckpts, held, examples), F32),
            pltpu.VMEM((ckpts, examples, lanes), F32),
        ],
        compiler_params=pltpu.CompilerParams(vmem_limit_bytes=12 << 20),
        name="scores",
    )(weight, feat, *holds)


def finish_kernel(*refs):
    pieces, out_ref = refs[:-1], refs[-1]
    held = out_ref.shape[1]
    result = jnp.zeros(out_ref.shape, F32)
    for c in range(pieces[0].shape[0]):
        total = pieces[0][c]
        for piece in pieces[1:]:
            total = total + piece[c]
        result = result + total[:, :held] * lax.rsqrt(total[:, held : held + 1] + 1e-06)
    out_ref[...] = result


def place_kernel(*refs, turn):
    block_ref, out_ref, sem = refs[0], refs[-2], refs[-1]
    copy = pltpu.make_async_copy(block_ref, out_ref.at[:, turn], sem)
    copy.start()
    copy.wait()


def together(blocks):
    ckpts, *rest = blocks[0].shape
    anywhere = pl.BlockSpec(memory_space=pl.ANY)
    joined = ()
    for turn, block in enumerate(blocks):
        if turn == 0:
            block = pltpu.with_memory_space_constraint(block, pltpu.HBM)
        joined = (
            pl.pallas_call(
                functools.partial(place_kernel, turn=turn),
                out_shape=jax.ShapeDtypeStruct((ckpts, len(blocks), *rest), block.dtype),
                in_specs=[anywhere] * (1 + len(joined)),
                out_specs=anywhere,
                scratch_shapes=[pltpu.SemaphoreType.DMA],
                input_output_aliases={1: 0} if joined else {},
                compiler_params=pltpu.CompilerParams(vmem_limit_bytes=12 << 20),
                cost_estimate=pl.CostEstimate(
                    flops=10_000_000_000, bytes_accessed=700_000, transcendentals=0
                ),
                name=f"place{turn}",
            )(block, *joined),
        )
    return joined[0]


def solution(mesh):
    parts = mesh.shape["layer"]
    peers = mesh.shape["dp"]

    def local(grad, act, var, hold, lengths, mask, seed, weight):
        ckpts, _, examples, slots, width = grad.shape
        rank = act.shape[-1]
        cols = hold.shape[-1] // rank
        members = 2 if peers % 2 == 0 else 1
        groups = peers // members
        gathered = [hold[:, 0]]
        for turn in range(1, members):
            ring = [
                (i, i // members * members + (i + members - turn) % members) for i in range(peers)
            ]
            gathered.append(lax.ppermute(hold[:, 0], "dp", ring))
        own = together(gathered)
        holds = [own]
        for step in range(1, groups):
            ring = [
                (i, target(i // members, step, groups) * members + i % members) for i in range(peers)
            ]
            holds.append(lax.ppermute(own, "dp", ring))
        feat = features_of(
            seed,
            lengths,
            mask.T,
            act.reshape(ckpts, examples * slots, rank),
            grad.reshape(ckpts, examples * slots, width),
            var[:, 0],
            cols,
        )
        pieces = list(scores_of(weight, feat, holds, parts))
        for step in range(1, parts):
            ring = [(i, (i + step) % parts) for i in range(parts)]
            pieces[step] = lax.ppermute(pieces[step], "layer", ring)
        vmem = pl.BlockSpec(memory_space=pltpu.VMEM)
        return pl.pallas_call(
            finish_kernel,
            out_shape=jax.ShapeDtypeStruct((examples // parts, peers * hold.shape[2]), F32),
            in_specs=[vmem] * parts,
            out_specs=vmem,
            compiler_params=pltpu.CompilerParams(vmem_limit_bytes=12 << 20),
            name="finish",
        )(*pieces)

    placed = (
        P(None, "layer", "dp", None, None),
        P(None, "layer", "dp", None, None),
        P(None, "layer", None, None),
        P(None, "layer", "dp", None),
        P("dp"),
        P("dp", None),
        P(),
        P(),
    )
    return jax.shard_map(
        local, mesh=mesh, in_specs=placed, out_specs=P(("dp", "layer"), None), check_vma=False
    )
```

```python
import functools
import math

import jax
import jax.numpy as jnp
from jax import lax
from jax.experimental import pallas as pl
from jax.experimental.pallas import tpu as pltpu
from jax.sharding import PartitionSpec as P

F32 = jnp.float32
BF16 = jnp.bfloat16
TILE = 256
LANES = 128
AHEAD = 2
READY = 2


def target(index, step, size):
    return index ^ step if size & (size - 1) == 0 else (index + step) % size


def source(index, step, size):
    return index ^ step if size & (size - 1) == 0 else (index + size - step) % size


def feature_kernel(
    seed_ref,
    len_ref,
    mask_ref,
    act_ref,
    grad_raw,
    var_raw,
    out_ref,
    lhs_ring,
    scale_ring,
    sign_ring,
    act_blocks,
    feat_buf,
    *,
    ckpts,
    examples,
    slots,
    width,
    cols,
    tiles,
):
    chunk = tiles * TILE
    chunks = width // chunk
    total = ckpts * chunks
    pairs = examples // 2
    per_unit = pairs // 2
    sign_rows = sign_ring.shape[0]
    inv_root = 1.0 / math.sqrt(width)

    hash_base = (
        lax.axis_index("layer") * jnp.int32(668265263) + seed_ref[0] * jnp.int32(374761393)
    )
    slot_ids = lax.broadcasted_iota(jnp.int32, (slots, 1), 0)
    for pair in range(pairs):
        marks = [
            (mask_ref[:, e : e + 1] == 1) & (slot_ids < len_ref[e])
            for e in (2 * pair, 2 * pair + 1)
        ]
        for c in range(ckpts):
            at = 2 * pair * slots
            first = jnp.where(marks[0], act_ref[c, at : at + slots, :].astype(F32), 0.0)
            second = jnp.where(marks[1], act_ref[c, at + slots : at + 2 * slots, :].astype(F32), 0.0)
            blank = jnp.zeros_like(first)
            act_blocks[c * pairs + pair] = jnp.concatenate(
                [jnp.concatenate([first, blank], 1), jnp.concatenate([blank, second], 1)], 0
            ).astype(BF16)

    def prepare(it, t, part):
        c, q = it // chunks, it % chunks
        base = q * chunk + t * TILE
        here = t * TILE
        if part < 2:
            half = part * LANES
            src = grad_raw[c, :, pl.ds(pl.multiple_of(base + half, LANES), LANES)]
            lhs_ring[here + half : here + half + LANES, :] = jnp.transpose(src)
        elif part == 2:
            moment = var_raw[c, pl.ds(pl.multiple_of(base, TILE), TILE), :].astype(F32)
            scale_ring[here : here + TILE, :] = 1.0 / (jnp.sqrt(moment) + 1e-08)
        else:
            d = lax.broadcasted_iota(jnp.int32, (sign_rows, TILE), 1) + base
            k = lax.broadcasted_iota(jnp.int32, (sign_rows, TILE), 0)
            m = d * jnp.int32(1103515245) + k * jnp.int32(12345) + hash_base
            m = m ^ (m >> 15)
            m = m * jnp.int32(747796405)
            m = m ^ (m >> 13)
            sign = (2 * ((m >> 7) & 1) - 1).astype(F32)
            sign_ring[:, here : here + TILE] = jnp.where(k < cols, sign, 0.0).astype(BF16)

    for t in range(READY):
        for part in range(4):
            prepare(0, t, part)

    def scoped(*accs):
        depth = AHEAD + 1
        outer_acc = [accs[m * depth : (m + 1) * depth] for m in (0, 1)]
        proj_acc = [accs[2 * depth + m * per_unit : 2 * depth + (m + 1) * per_unit] for m in (0, 1)]
        steps = [(t, j) for t in range(tiles) for j in range(per_unit)]

        def outer(c, m, n):
            t, j = steps[n]
            tokens = lhs_ring[t * TILE : (t + 1) * TILE, :]
            pair = m * per_unit + j
            sizes = (2 * slots * pair, TILE - 2 * slots * (pair + 1))
            above, below = ([jnp.zeros((n, TILE), BF16)] if n else [] for n in sizes)
            block = [*above, act_blocks[c * pairs + pair], *below]
            pltpu.matmul_push_rhs(jnp.concatenate(block, 0), 0, m)
            pltpu.matmul_acc_lhs(
                outer_acc[m][n % depth], jnp.concatenate([tokens, tokens], 1), load_staged_rhs=0
            )

        def project(m, n):
            t, j = steps[n]
            at = slice(t * TILE, (t + 1) * TILE)
            summed = pltpu.matmul_pop(outer_acc[m][n % depth])
            scale = scale_ring[at, :]
            scaled = (summed * jnp.concatenate([scale, scale], 1)).astype(BF16)
            pltpu.matmul_push_rhs(scaled, 1, m)
            pltpu.matmul_acc_lhs(proj_acc[m][j], sign_ring[:, at], load_staged_rhs=1)

        def one_chunk(c, q):
            it = c * chunks + q
            following = jnp.minimum(it + 1, total - 1)

            for n in range(1, AHEAD):
                for m in (0, 1):
                    outer(c, m, n)
            for n in range(len(steps)):
                for m in (0, 1):
                    if n + AHEAD < len(steps):
                        outer(c, m, n + AHEAD)
                    project(m, n)
                    if n == len(steps) - 2:
                        outer(following // chunks, m, 0)
                t, j = steps[n]
                for part in range(j * 4 // per_unit, (j + 1) * 4 // per_unit):
                    if t + READY < tiles:
                        prepare(it, t + READY, part)
                    else:
                        prepare(following, t + READY - tiles, part)

        def one_ckpt(c, carry):
            def body(q, inner):
                one_chunk(c, q)
                return inner

            lax.fori_loop(0, chunks, body, 0)
            for m in (0, 1):
                for j in range(per_unit):
                    total_sum = pltpu.matmul_pop(proj_acc[m][j])
                    for half in range(2):
                        e = 2 * (m * per_unit + j) + half
                        feat_buf[e] = total_sum[:cols, half * LANES : (half + 1) * LANES] * inv_root
            for k in range(cols):
                out_ref[c, :, k * LANES : (k + 1) * LANES] = feat_buf[:, k, :].astype(BF16)
            return carry

        for m in (0, 1):
            outer(0, m, 0)
        lax.fori_loop(0, ckpts, one_ckpt, 0)
        for m in (0, 1):
            pltpu.matmul_pop(outer_acc[m][0])

    pl.run_scoped(
        scoped,
        *[pltpu.ACC(m)((TILE, TILE), F32) for m in (0, 1) for _ in range(AHEAD + 1)],
        *[pltpu.ACC(m)((sign_rows, TILE), F32) for m in (0, 1) for _ in range(per_unit)],
    )


def features_of(seed, lengths, mask, act, grad, var, cols):
    ckpts, rows, width = grad.shape
    slots, examples = mask.shape
    tiles = 8
    chunk = tiles * TILE
    pairs = examples // 2
    sign_rows = -(-cols // 16) * 16
    vmem = pl.BlockSpec(memory_space=pltpu.VMEM)
    smem = pl.BlockSpec(memory_space=pltpu.SMEM)
    kernel = functools.partial(
        feature_kernel,
        ckpts=ckpts,
        examples=examples,
        slots=slots,
        width=width,
        cols=cols,
        tiles=tiles,
    )
    return pl.pallas_call(
        kernel,
        out_shape=jax.ShapeDtypeStruct((ckpts, examples, cols * LANES), BF16),
        in_specs=[smem, smem] + [vmem] * 4,
        out_specs=vmem,
        scratch_shapes=[
            pltpu.VMEM((chunk, LANES), BF16),
            pltpu.VMEM((chunk, LANES), F32),
            pltpu.VMEM((sign_rows, chunk), BF16),
            pltpu.VMEM((ckpts * pairs, 2 * slots, TILE), BF16),
            pltpu.VMEM((examples, cols, LANES), F32),
        ],
        compiler_params=pltpu.CompilerParams(vmem_limit_bytes=24 << 20),
        cost_estimate=pl.CostEstimate(
            flops=40_000_000_000, bytes_accessed=9_000_000, transcendentals=0
        ),
        name="features",
    )(seed, lengths, mask, act, grad, var)


def score_kernel(*refs, groups, parts):
    weight_ref, feat_ref, holds = refs[0], refs[1], refs[2 : 2 + groups]
    outs, (turned, sums) = refs[2 + groups : 2 + groups + parts], refs[2 + groups + parts :]
    ckpts, examples, width = feat_ref.shape
    members, block = holds[0].shape[1:3]
    held = groups * members * block
    share = examples // parts
    mine = lax.axis_index("dp")
    me = lax.axis_index("layer")
    group, member = mine // members, lax.rem(mine, members)
    for c in range(ckpts):
        feat = feat_ref[c]
        stack = jnp.concatenate([hold[c].reshape(members * block, width) for hold in holds], 0)
        found = lax.dot_general(
            stack, feat, (((1,), (1,)), ((), ())), preferred_element_type=F32
        )
        for step in range(groups):
            first = source(group, step, groups) * members
            for turn in range(members):
                index = first + lax.rem(member + turn, members)
                at = (step * members + turn) * block
                turned[c, pl.ds(pl.multiple_of(index * block, block), block), :] = found[
                    at : at + block
                ]
        wide = feat.astype(F32)
        norm = jnp.sum(wide * wide, axis=1, keepdims=True)
        sums[c, :, :held] = jnp.transpose(turned[c]) * weight_ref[c]
        sums[c, :, held:] = jnp.broadcast_to(norm, (examples, sums.shape[2] - held))
        for step in range(parts):
            owner = lax.rem(me + step, parts)
            outs[step][c] = sums[c, pl.ds(owner * share, share), :]


def scores_of(weight, feat, holds, parts):
    ckpts, examples, width = feat.shape
    groups = len(holds)
    members, block = holds[0].shape[1:3]
    held = groups * members * block
    lanes = (held // LANES + 1) * LANES
    vmem = pl.BlockSpec(memory_space=pltpu.VMEM)
    return pl.pallas_call(
        functools.partial(score_kernel, groups=groups, parts=parts),
        out_shape=[jax.ShapeDtypeStruct((ckpts, examples // parts, lanes), F32)] * parts,
        in_specs=[pl.BlockSpec(memory_space=pltpu.SMEM)] + [vmem] * (1 + groups),
        out_specs=[vmem] * parts,
        scratch_shapes=[
            pltpu.VMEM((ckpts, held, examples), F32),
            pltpu.VMEM((ckpts, examples, lanes), F32),
        ],
        compiler_params=pltpu.CompilerParams(vmem_limit_bytes=12 << 20),
        name="scores",
    )(weight, feat, *holds)


def finish_kernel(*refs):
    pieces, out_ref = refs[:-1], refs[-1]
    held = out_ref.shape[1]
    result = jnp.zeros(out_ref.shape, F32)
    for c in range(pieces[0].shape[0]):
        total = pieces[0][c]
        for piece in pieces[1:]:
            total = total + piece[c]
        result = result + total[:, :held] * lax.rsqrt(total[:, held : held + 1] + 1e-06)
    out_ref[...] = result


def place_kernel(*refs, turn):
    block_ref, out_ref, sem = refs[0], refs[-2], refs[-1]
    copy = pltpu.make_async_copy(block_ref, out_ref.at[:, turn], sem)
    copy.start()
    copy.wait()


def together(blocks):
    ckpts, *rest = blocks[0].shape
    anywhere = pl.BlockSpec(memory_space=pl.ANY)
    joined = ()
    for turn, block in enumerate(blocks):
        if turn == 0:
            block = pltpu.with_memory_space_constraint(block, pltpu.HBM)
        joined = (
            pl.pallas_call(
                functools.partial(place_kernel, turn=turn),
                out_shape=jax.ShapeDtypeStruct((ckpts, len(blocks), *rest), block.dtype),
                in_specs=[anywhere] * (1 + len(joined)),
                out_specs=anywhere,
                scratch_shapes=[pltpu.SemaphoreType.DMA],
                input_output_aliases={1: 0} if joined else {},
                compiler_params=pltpu.CompilerParams(vmem_limit_bytes=12 << 20),
                cost_estimate=pl.CostEstimate(
                    flops=10_000_000_000, bytes_accessed=700_000, transcendentals=0
                ),
                name=f"place{turn}",
            )(block, *joined),
        )
    return joined[0]


def solution(mesh):
    parts = mesh.shape["layer"]
    peers = mesh.shape["dp"]

    def local(grad, act, var, hold, lengths, mask, seed, weight):
        ckpts, _, examples, slots, width = grad.shape
        rank = act.shape[-1]
        cols = hold.shape[-1] // rank
        members = 2 if peers % 2 == 0 else 1
        groups = peers // members
        gathered = [hold[:, 0]]
        for turn in range(1, members):
            ring = [
                (i, i // members * members + (i + members - turn) % members) for i in range(peers)
            ]
            gathered.append(lax.ppermute(hold[:, 0], "dp", ring))
        own = together(gathered)
        holds = [own]
        for step in range(1, groups):
            ring = [
                (i, target(i // members, step, groups) * members + i % members) for i in range(peers)
            ]
            holds.append(lax.ppermute(own, "dp", ring))
        feat = features_of(
            seed,
            lengths,
            mask.T,
            act.reshape(ckpts, examples * slots, rank),
            grad.reshape(ckpts, examples * slots, width),
            var[:, 0],
            cols,
        )
        pieces = list(scores_of(weight, feat, holds, parts))
        for step in range(1, parts):
            ring = [(i, (i + step) % parts) for i in range(parts)]
            pieces[step] = lax.ppermute(pieces[step], "layer", ring)
        vmem = pl.BlockSpec(memory_space=pltpu.VMEM)
        return pl.pallas_call(
            finish_kernel,
            out_shape=jax.ShapeDtypeStruct((examples // parts, peers * hold.shape[2]), F32),
            in_specs=[vmem] * parts,
            out_specs=vmem,
            compiler_params=pltpu.CompilerParams(vmem_limit_bytes=12 << 20),
            name="finish",
        )(*pieces)

    placed = (
        P(None, "layer", "dp", None, None),
        P(None, "layer", "dp", None, None),
        P(None, "layer", None, None),
        P(None, "layer", "dp", None),
        P("dp"),
        P("dp", None),
        P(),
        P(),
    )
    return jax.shard_map(
        local, mesh=mesh, in_specs=placed, out_specs=P(("dp", "layer"), None), check_vma=False
    )
```

```python
import functools
import math

import jax
import jax.numpy as jnp
from jax import lax
from jax.experimental import pallas as pl
from jax.experimental.pallas import tpu as pltpu
from jax.sharding import PartitionSpec as P

F32 = jnp.float32
BF16 = jnp.bfloat16
TILE = 256
LANES = 128
AHEAD = 2
READY = 2


def target(index, step, size):
    return index ^ step if size & (size - 1) == 0 else (index + step) % size


def source(index, step, size):
    return index ^ step if size & (size - 1) == 0 else (index + size - step) % size


def feature_kernel(
    seed_ref,
    len_ref,
    mask_ref,
    act_ref,
    grad_raw,
    var_raw,
    out_ref,
    lhs_ring,
    scale_ring,
    sign_ring,
    act_blocks,
    feat_buf,
    *,
    ckpts,
    examples,
    slots,
    width,
    cols,
    tiles,
):
    chunk = tiles * TILE
    chunks = width // chunk
    total = ckpts * chunks
    pairs = examples // 2
    per_unit = pairs // 2
    sign_rows = sign_ring.shape[0]
    inv_root = 1.0 / math.sqrt(width)

    hash_base = (
        lax.axis_index("layer") * jnp.int32(668265263) + seed_ref[0] * jnp.int32(374761393)
    )
    slot_ids = lax.broadcasted_iota(jnp.int32, (slots, examples), 0)
    valid = jnp.where((mask_ref[...] == 1) & (slot_ids < len_ref[...]), 1.0, 0.0)
    for pair in range(pairs):
        marks = [valid[:, e : e + 1] > 0.5 for e in (2 * pair, 2 * pair + 1)]
        for c in range(ckpts):
            at = 2 * pair * slots
            first = jnp.where(marks[0], act_ref[c, at : at + slots, :].astype(F32), 0.0)
            second = jnp.where(marks[1], act_ref[c, at + slots : at + 2 * slots, :].astype(F32), 0.0)
            blank = jnp.zeros_like(first)
            act_blocks[c * pairs + pair] = jnp.concatenate(
                [jnp.concatenate([first, blank], 1), jnp.concatenate([blank, second], 1)], 0
            ).astype(BF16)

    def prepare(it, t, part):
        c, q = it // chunks, it % chunks
        base = q * chunk + t * TILE
        here = t * TILE
        if part < 2:
            half = part * LANES
            src = grad_raw[c, :, pl.ds(pl.multiple_of(base + half, LANES), LANES)]
            lhs_ring[here + half : here + half + LANES, :] = jnp.transpose(src)
        elif part == 2:
            moment = var_raw[c, pl.ds(pl.multiple_of(base, TILE), TILE), :].astype(F32)
            scale_ring[here : here + TILE, :] = 1.0 / (jnp.sqrt(moment) + 1e-08)
        else:
            d = lax.broadcasted_iota(jnp.int32, (sign_rows, TILE), 1) + base
            k = lax.broadcasted_iota(jnp.int32, (sign_rows, TILE), 0)
            m = d * jnp.int32(1103515245) + k * jnp.int32(12345) + hash_base
            m = m ^ (m >> 15)
            m = m * jnp.int32(747796405)
            m = m ^ (m >> 13)
            sign = (2 * ((m >> 7) & 1) - 1).astype(F32)
            sign_ring[:, here : here + TILE] = jnp.where(k < cols, sign, 0.0).astype(BF16)

    for t in range(READY):
        for part in range(4):
            prepare(0, t, part)

    def scoped(*accs):
        depth = AHEAD + 1
        outer_acc = [accs[m * depth : (m + 1) * depth] for m in (0, 1)]
        proj_acc = [accs[2 * depth + m * per_unit : 2 * depth + (m + 1) * per_unit] for m in (0, 1)]
        steps = [(t, j) for t in range(tiles) for j in range(per_unit)]

        def outer(c, m, n):
            t, j = steps[n]
            tokens = lhs_ring[t * TILE : (t + 1) * TILE, :]
            pair = m * per_unit + j
            sizes = (2 * slots * pair, TILE - 2 * slots * (pair + 1))
            above, below = ([jnp.zeros((n, TILE), BF16)] if n else [] for n in sizes)
            block = [*above, act_blocks[c * pairs + pair], *below]
            pltpu.matmul_push_rhs(jnp.concatenate(block, 0), 0, m)
            pltpu.matmul_acc_lhs(
                outer_acc[m][n % depth], jnp.concatenate([tokens, tokens], 1), load_staged_rhs=0
            )

        def project(m, n):
            t, j = steps[n]
            at = slice(t * TILE, (t + 1) * TILE)
            summed = pltpu.matmul_pop(outer_acc[m][n % depth])
            scale = scale_ring[at, :]
            scaled = (summed * jnp.concatenate([scale, scale], 1)).astype(BF16)
            pltpu.matmul_push_rhs(scaled, 1, m)
            pltpu.matmul_acc_lhs(proj_acc[m][j], sign_ring[:, at], load_staged_rhs=1)

        def one_chunk(c, q):
            it = c * chunks + q
            following = jnp.minimum(it + 1, total - 1)

            for n in range(1, AHEAD):
                for m in (0, 1):
                    outer(c, m, n)
            for n in range(len(steps)):
                for m in (0, 1):
                    if n + AHEAD < len(steps):
                        outer(c, m, n + AHEAD)
                    project(m, n)
                    if n == len(steps) - 2:
                        outer(following // chunks, m, 0)
                t, j = steps[n]
                for part in range(j * 4 // per_unit, (j + 1) * 4 // per_unit):
                    if t + READY < tiles:
                        prepare(it, t + READY, part)
                    else:
                        prepare(following, t + READY - tiles, part)

        def one_ckpt(c, carry):
            def body(q, inner):
                one_chunk(c, q)
                return inner

            lax.fori_loop(0, chunks, body, 0)
            for m in (0, 1):
                for j in range(per_unit):
                    total_sum = pltpu.matmul_pop(proj_acc[m][j])
                    for half in range(2):
                        e = 2 * (m * per_unit + j) + half
                        feat_buf[e] = total_sum[:cols, half * LANES : (half + 1) * LANES] * inv_root
            for k in range(cols):
                out_ref[c, :, k * LANES : (k + 1) * LANES] = feat_buf[:, k, :].astype(BF16)
            return carry

        for m in (0, 1):
            outer(0, m, 0)
        lax.fori_loop(0, ckpts, one_ckpt, 0)
        for m in (0, 1):
            pltpu.matmul_pop(outer_acc[m][0])

    pl.run_scoped(
        scoped,
        *[pltpu.ACC(m)((TILE, TILE), F32) for m in (0, 1) for _ in range(AHEAD + 1)],
        *[pltpu.ACC(m)((sign_rows, TILE), F32) for m in (0, 1) for _ in range(per_unit)],
    )


def features_of(seed, lengths, mask, act, grad, var, cols):
    ckpts, rows, width = grad.shape
    slots, examples = mask.shape
    tiles = 8
    chunk = tiles * TILE
    pairs = examples // 2
    sign_rows = -(-cols // 16) * 16
    vmem = pl.BlockSpec(memory_space=pltpu.VMEM)
    smem = pl.BlockSpec(memory_space=pltpu.SMEM)
    kernel = functools.partial(
        feature_kernel,
        ckpts=ckpts,
        examples=examples,
        slots=slots,
        width=width,
        cols=cols,
        tiles=tiles,
    )
    return pl.pallas_call(
        kernel,
        out_shape=jax.ShapeDtypeStruct((ckpts, examples, cols * LANES), BF16),
        in_specs=[smem] + [vmem] * 5,
        out_specs=vmem,
        scratch_shapes=[
            pltpu.VMEM((chunk, LANES), BF16),
            pltpu.VMEM((chunk, LANES), F32),
            pltpu.VMEM((sign_rows, chunk), BF16),
            pltpu.VMEM((ckpts * pairs, 2 * slots, TILE), BF16),
            pltpu.VMEM((examples, cols, LANES), F32),
        ],
        compiler_params=pltpu.CompilerParams(vmem_limit_bytes=24 << 20),
        cost_estimate=pl.CostEstimate(
            flops=40_000_000_000, bytes_accessed=9_000_000, transcendentals=0
        ),
        name="features",
    )(seed, lengths, mask, act, grad, var)


def score_kernel(*refs, groups, parts):
    weight_ref, feat_ref, holds = refs[0], refs[1], refs[2 : 2 + groups]
    outs, (turned, sums) = refs[2 + groups : 2 + groups + parts], refs[2 + groups + parts :]
    ckpts, examples, width = feat_ref.shape
    members, block = holds[0].shape[1:3]
    held = groups * members * block
    share = examples // parts
    mine = lax.axis_index("dp")
    me = lax.axis_index("layer")
    group, member = mine // members, lax.rem(mine, members)
    for c in range(ckpts):
        feat = feat_ref[c]
        stack = jnp.concatenate([hold[c].reshape(members * block, width) for hold in holds], 0)
        found = lax.dot_general(
            stack, feat, (((1,), (1,)), ((), ())), preferred_element_type=F32
        )
        for step in range(groups):
            first = source(group, step, groups) * members
            for turn in range(members):
                index = first + lax.rem(member + turn, members)
                at = (step * members + turn) * block
                turned[c, pl.ds(pl.multiple_of(index * block, block), block), :] = found[
                    at : at + block
                ]
        wide = feat.astype(F32)
        norm = jnp.sum(wide * wide, axis=1, keepdims=True)
        sums[c, :, :held] = jnp.transpose(turned[c]) * weight_ref[:, c : c + 1]
        sums[c, :, held:] = jnp.broadcast_to(norm, (examples, sums.shape[2] - held))
        for step in range(parts):
            owner = lax.rem(me + step, parts)
            outs[step][c] = sums[c, pl.ds(owner * share, share), :]


def scores_of(weight, feat, holds, parts):
    ckpts, examples, width = feat.shape
    groups = len(holds)
    members, block = holds[0].shape[1:3]
    held = groups * members * block
    lanes = (held // LANES + 1) * LANES
    vmem = pl.BlockSpec(memory_space=pltpu.VMEM)
    return pl.pallas_call(
        functools.partial(score_kernel, groups=groups, parts=parts),
        out_shape=[jax.ShapeDtypeStruct((ckpts, examples // parts, lanes), F32)] * parts,
        in_specs=[vmem] * (2 + groups),
        out_specs=[vmem] * parts,
        scratch_shapes=[
            pltpu.VMEM((ckpts, held, examples), F32),
            pltpu.VMEM((ckpts, examples, lanes), F32),
        ],
        compiler_params=pltpu.CompilerParams(vmem_limit_bytes=12 << 20),
        name="scores",
    )(weight, feat, *holds)


def finish_kernel(*refs):
    pieces, out_ref = refs[:-1], refs[-1]
    held = out_ref.shape[1]
    result = jnp.zeros(out_ref.shape, F32)
    for c in range(pieces[0].shape[0]):
        total = pieces[0][c]
        for piece in pieces[1:]:
            total = total + piece[c]
        result = result + total[:, :held] * lax.rsqrt(total[:, held : held + 1] + 1e-06)
    out_ref[...] = result


def place_kernel(*refs, turn):
    block_ref, out_ref, sem = refs[0], refs[-2], refs[-1]
    copy = pltpu.make_async_copy(block_ref, out_ref.at[:, turn], sem)
    copy.start()
    copy.wait()


def together(blocks):
    ckpts, *rest = blocks[0].shape
    anywhere = pl.BlockSpec(memory_space=pl.ANY)
    joined = ()
    for turn, block in enumerate(blocks):
        if turn == 0:
            block = pltpu.with_memory_space_constraint(block, pltpu.HBM)
        joined = (
            pl.pallas_call(
                functools.partial(place_kernel, turn=turn),
                out_shape=jax.ShapeDtypeStruct((ckpts, len(blocks), *rest), block.dtype),
                in_specs=[anywhere] * (1 + len(joined)),
                out_specs=anywhere,
                scratch_shapes=[pltpu.SemaphoreType.DMA],
                input_output_aliases={1: 0} if joined else {},
                compiler_params=pltpu.CompilerParams(vmem_limit_bytes=12 << 20),
                cost_estimate=pl.CostEstimate(
                    flops=10_000_000_000, bytes_accessed=700_000, transcendentals=0
                ),
                name=f"place{turn}",
            )(block, *joined),
        )
    return joined[0]


def solution(mesh):
    parts = mesh.shape["layer"]
    peers = mesh.shape["dp"]

    def local(grad, act, var, hold, lengths, mask, seed, weight):
        ckpts, _, examples, slots, width = grad.shape
        rank = act.shape[-1]
        cols = hold.shape[-1] // rank
        members = 2 if peers % 2 == 0 else 1
        groups = peers // members
        gathered = [hold[:, 0]]
        for turn in range(1, members):
            ring = [
                (i, i // members * members + (i + members - turn) % members) for i in range(peers)
            ]
            gathered.append(lax.ppermute(hold[:, 0], "dp", ring))
        own = together(gathered)
        holds = [own]
        for step in range(1, groups):
            ring = [
                (i, target(i // members, step, groups) * members + i % members) for i in range(peers)
            ]
            holds.append(lax.ppermute(own, "dp", ring))
        feat = features_of(
            seed,
            lengths[None, :],
            mask.T,
            act.reshape(ckpts, examples * slots, rank),
            grad.reshape(ckpts, examples * slots, width),
            var[:, 0],
            cols,
        )
        pieces = list(scores_of(weight[None, :], feat, holds, parts))
        for step in range(1, parts):
            ring = [(i, (i + step) % parts) for i in range(parts)]
            pieces[step] = lax.ppermute(pieces[step], "layer", ring)
        vmem = pl.BlockSpec(memory_space=pltpu.VMEM)
        return pl.pallas_call(
            finish_kernel,
            out_shape=jax.ShapeDtypeStruct((examples // parts, peers * hold.shape[2]), F32),
            in_specs=[vmem] * parts,
            out_specs=vmem,
            compiler_params=pltpu.CompilerParams(vmem_limit_bytes=12 << 20),
            name="finish",
        )(*pieces)

    placed = (
        P(None, "layer", "dp", None, None),
        P(None, "layer", "dp", None, None),
        P(None, "layer", None, None),
        P(None, "layer", "dp", None),
        P("dp"),
        P("dp", None),
        P(),
        P(),
    )
    return jax.shard_map(
        local, mesh=mesh, in_specs=placed, out_specs=P(("dp", "layer"), None), check_vma=False
    )
```

```python
import functools
import math

import jax
import jax.numpy as jnp
from jax import lax
from jax.experimental import pallas as pl
from jax.experimental.pallas import tpu as pltpu
from jax.sharding import PartitionSpec as P

F32 = jnp.float32
BF16 = jnp.bfloat16
TILE = 256
LANES = 128
AHEAD = 2
READY = 1


def target(index, step, size):
    return index ^ step if size & (size - 1) == 0 else (index + step) % size


def source(index, step, size):
    return index ^ step if size & (size - 1) == 0 else (index + size - step) % size


def feature_kernel(
    seed_ref,
    len_ref,
    mask_ref,
    act_ref,
    grad_raw,
    var_raw,
    out_ref,
    lhs_ring,
    scale_ring,
    sign_ring,
    act_blocks,
    feat_buf,
    *,
    ckpts,
    examples,
    slots,
    width,
    cols,
    tiles,
):
    chunk = tiles * TILE
    chunks = width // chunk
    total = ckpts * chunks
    pairs = examples // 2
    per_unit = pairs // 2
    sign_rows = sign_ring.shape[0]
    inv_root = 1.0 / math.sqrt(width)

    hash_base = (
        lax.axis_index("layer") * jnp.int32(668265263) + seed_ref[0] * jnp.int32(374761393)
    )
    slot_ids = lax.broadcasted_iota(jnp.int32, (slots, examples), 0)
    valid = jnp.where((mask_ref[...] == 1) & (slot_ids < len_ref[...]), 1.0, 0.0)
    for pair in range(pairs):
        marks = [valid[:, e : e + 1] > 0.5 for e in (2 * pair, 2 * pair + 1)]
        for c in range(ckpts):
            at = 2 * pair * slots
            first = jnp.where(marks[0], act_ref[c, at : at + slots, :].astype(F32), 0.0)
            second = jnp.where(marks[1], act_ref[c, at + slots : at + 2 * slots, :].astype(F32), 0.0)
            blank = jnp.zeros_like(first)
            act_blocks[c * pairs + pair] = jnp.concatenate(
                [jnp.concatenate([first, blank], 1), jnp.concatenate([blank, second], 1)], 0
            ).astype(BF16)

    def prepare(it, t, part):
        c, q = it // chunks, it % chunks
        base = q * chunk + t * TILE
        here = t * TILE
        if part < 2:
            half = part * LANES
            src = grad_raw[c, :, pl.ds(pl.multiple_of(base + half, LANES), LANES)]
            lhs_ring[here + half : here + half + LANES, :] = jnp.transpose(src)
        elif part == 2:
            moment = var_raw[c, pl.ds(pl.multiple_of(base, TILE), TILE), :].astype(F32)
            scale_ring[here : here + TILE, :] = 1.0 / (jnp.sqrt(moment) + 1e-08)
        else:
            d = lax.broadcasted_iota(jnp.int32, (sign_rows, TILE), 1) + base
            k = lax.broadcasted_iota(jnp.int32, (sign_rows, TILE), 0)
            m = d * jnp.int32(1103515245) + k * jnp.int32(12345) + hash_base
            m = m ^ (m >> 15)
            m = m * jnp.int32(747796405)
            m = m ^ (m >> 13)
            sign = (2 * ((m >> 7) & 1) - 1).astype(F32)
            sign_ring[:, here : here + TILE] = jnp.where(k < cols, sign, 0.0).astype(BF16)

    for t in range(READY):
        for part in range(4):
            prepare(0, t, part)

    def scoped(*accs):
        depth = AHEAD + 1
        outer_acc = [accs[m * depth : (m + 1) * depth] for m in (0, 1)]
        proj_acc = [accs[2 * depth + m * per_unit : 2 * depth + (m + 1) * per_unit] for m in (0, 1)]
        steps = [(t, j) for t in range(tiles) for j in range(per_unit)]

        def outer(c, m, n):
            t, j = steps[n]
            tokens = lhs_ring[t * TILE : (t + 1) * TILE, :]
            pair = m * per_unit + j
            sizes = (2 * slots * pair, TILE - 2 * slots * (pair + 1))
            above, below = ([jnp.zeros((n, TILE), BF16)] if n else [] for n in sizes)
            block = [*above, act_blocks[c * pairs + pair], *below]
            pltpu.matmul_push_rhs(jnp.concatenate(block, 0), 0, m)
            pltpu.matmul_acc_lhs(
                outer_acc[m][n % depth], jnp.concatenate([tokens, tokens], 1), load_staged_rhs=0
            )

        def project(m, n):
            t, j = steps[n]
            at = slice(t * TILE, (t + 1) * TILE)
            summed = pltpu.matmul_pop(outer_acc[m][n % depth])
            scale = scale_ring[at, :]
            scaled = (summed * jnp.concatenate([scale, scale], 1)).astype(BF16)
            pltpu.matmul_push_rhs(scaled, 1, m)
            pltpu.matmul_acc_lhs(proj_acc[m][j], sign_ring[:, at], load_staged_rhs=1)

        def one_chunk(c, q):
            it = c * chunks + q
            following = jnp.minimum(it + 1, total - 1)

            for n in range(1, AHEAD):
                for m in (0, 1):
                    outer(c, m, n)
            for n in range(len(steps)):
                for m in (0, 1):
                    if n + AHEAD < len(steps):
                        outer(c, m, n + AHEAD)
                    project(m, n)
                    if n == len(steps) - 2:
                        outer(following // chunks, m, 0)
                t, j = steps[n]
                for part in range(j * 4 // per_unit, (j + 1) * 4 // per_unit):
                    if t + READY < tiles:
                        prepare(it, t + READY, part)
                    else:
                        prepare(following, t + READY - tiles, part)

        def one_ckpt(c, carry):
            def body(q, inner):
                one_chunk(c, q)
                return inner

            lax.fori_loop(0, chunks, body, 0)
            for m in (0, 1):
                for j in range(per_unit):
                    total_sum = pltpu.matmul_pop(proj_acc[m][j])
                    for half in range(2):
                        e = 2 * (m * per_unit + j) + half
                        feat_buf[e] = total_sum[:cols, half * LANES : (half + 1) * LANES] * inv_root
            for k in range(cols):
                out_ref[c, :, k * LANES : (k + 1) * LANES] = feat_buf[:, k, :].astype(BF16)
            return carry

        for m in (0, 1):
            outer(0, m, 0)
        lax.fori_loop(0, ckpts, one_ckpt, 0)
        for m in (0, 1):
            pltpu.matmul_pop(outer_acc[m][0])

    pl.run_scoped(
        scoped,
        *[pltpu.ACC(m)((TILE, TILE), F32) for m in (0, 1) for _ in range(AHEAD + 1)],
        *[pltpu.ACC(m)((sign_rows, TILE), F32) for m in (0, 1) for _ in range(per_unit)],
    )


def features_of(seed, lengths, mask, act, grad, var, cols):
    ckpts, rows, width = grad.shape
    slots, examples = mask.shape
    tiles = 8
    chunk = tiles * TILE
    pairs = examples // 2
    sign_rows = -(-cols // 16) * 16
    vmem = pl.BlockSpec(memory_space=pltpu.VMEM)
    smem = pl.BlockSpec(memory_space=pltpu.SMEM)
    kernel = functools.partial(
        feature_kernel,
        ckpts=ckpts,
        examples=examples,
        slots=slots,
        width=width,
        cols=cols,
        tiles=tiles,
    )
    return pl.pallas_call(
        kernel,
        out_shape=jax.ShapeDtypeStruct((ckpts, examples, cols * LANES), BF16),
        in_specs=[smem] + [vmem] * 5,
        out_specs=vmem,
        scratch_shapes=[
            pltpu.VMEM((chunk, LANES), BF16),
            pltpu.VMEM((chunk, LANES), F32),
            pltpu.VMEM((sign_rows, chunk), BF16),
            pltpu.VMEM((ckpts * pairs, 2 * slots, TILE), BF16),
            pltpu.VMEM((examples, cols, LANES), F32),
        ],
        compiler_params=pltpu.CompilerParams(vmem_limit_bytes=24 << 20),
        cost_estimate=pl.CostEstimate(
            flops=40_000_000_000, bytes_accessed=9_000_000, transcendentals=0
        ),
        name="features",
    )(seed, lengths, mask, act, grad, var)


def score_kernel(*refs, groups, parts):
    weight_ref, feat_ref, holds = refs[0], refs[1], refs[2 : 2 + groups]
    outs, (turned, sums) = refs[2 + groups : 2 + groups + parts], refs[2 + groups + parts :]
    ckpts, examples, width = feat_ref.shape
    members, block = holds[0].shape[1:3]
    held = groups * members * block
    share = examples // parts
    mine = lax.axis_index("dp")
    me = lax.axis_index("layer")
    group, member = mine // members, lax.rem(mine, members)
    for c in range(ckpts):
        feat = feat_ref[c]
        stack = jnp.concatenate([hold[c].reshape(members * block, width) for hold in holds], 0)
        found = lax.dot_general(
            stack, feat, (((1,), (1,)), ((), ())), preferred_element_type=F32
        )
        for step in range(groups):
            first = source(group, step, groups) * members
            for turn in range(members):
                index = first + lax.rem(member + turn, members)
                at = (step * members + turn) * block
                turned[c, pl.ds(pl.multiple_of(index * block, block), block), :] = found[
                    at : at + block
                ]
        wide = feat.astype(F32)
        norm = jnp.sum(wide * wide, axis=1, keepdims=True)
        sums[c, :, :held] = jnp.transpose(turned[c]) * weight_ref[:, c : c + 1]
        sums[c, :, held:] = jnp.broadcast_to(norm, (examples, sums.shape[2] - held))
        for step in range(parts):
            owner = lax.rem(me + step, parts)
            outs[step][c] = sums[c, pl.ds(owner * share, share), :]


def scores_of(weight, feat, holds, parts):
    ckpts, examples, width = feat.shape
    groups = len(holds)
    members, block = holds[0].shape[1:3]
    held = groups * members * block
    lanes = (held // LANES + 1) * LANES
    vmem = pl.BlockSpec(memory_space=pltpu.VMEM)
    return pl.pallas_call(
        functools.partial(score_kernel, groups=groups, parts=parts),
        out_shape=[jax.ShapeDtypeStruct((ckpts, examples // parts, lanes), F32)] * parts,
        in_specs=[vmem] * (2 + groups),
        out_specs=[vmem] * parts,
        scratch_shapes=[
            pltpu.VMEM((ckpts, held, examples), F32),
            pltpu.VMEM((ckpts, examples, lanes), F32),
        ],
        compiler_params=pltpu.CompilerParams(vmem_limit_bytes=12 << 20),
        name="scores",
    )(weight, feat, *holds)


def finish_kernel(*refs):
    pieces, out_ref = refs[:-1], refs[-1]
    held = out_ref.shape[1]
    result = jnp.zeros(out_ref.shape, F32)
    for c in range(pieces[0].shape[0]):
        total = pieces[0][c]
        for piece in pieces[1:]:
            total = total + piece[c]
        result = result + total[:, :held] * lax.rsqrt(total[:, held : held + 1] + 1e-06)
    out_ref[...] = result


def place_kernel(*refs, turn):
    block_ref, out_ref, sem = refs[0], refs[-2], refs[-1]
    copy = pltpu.make_async_copy(block_ref, out_ref.at[:, turn], sem)
    copy.start()
    copy.wait()


def together(blocks):
    ckpts, *rest = blocks[0].shape
    anywhere = pl.BlockSpec(memory_space=pl.ANY)
    joined = ()
    for turn, block in enumerate(blocks):
        joined = (
            pl.pallas_call(
                functools.partial(place_kernel, turn=turn),
                out_shape=jax.ShapeDtypeStruct((ckpts, len(blocks), *rest), block.dtype),
                in_specs=[anywhere] * (1 + len(joined)),
                out_specs=anywhere,
                scratch_shapes=[pltpu.SemaphoreType.DMA],
                input_output_aliases={1: 0} if joined else {},
                compiler_params=pltpu.CompilerParams(vmem_limit_bytes=12 << 20),
                cost_estimate=pl.CostEstimate(
                    flops=10_000_000_000, bytes_accessed=700_000, transcendentals=0
                ),
                name=f"place{turn}",
            )(block, *joined),
        )
    return joined[0]


def solution(mesh):
    parts = mesh.shape["layer"]
    peers = mesh.shape["dp"]

    def local(grad, act, var, hold, lengths, mask, seed, weight):
        ckpts, _, examples, slots, width = grad.shape
        rank = act.shape[-1]
        cols = hold.shape[-1] // rank
        members = 2 if peers % 2 == 0 else 1
        groups = peers // members
        gathered = [hold[:, 0]]
        for turn in range(1, members):
            ring = [
                (i, i // members * members + (i + members - turn) % members) for i in range(peers)
            ]
            gathered.append(lax.ppermute(hold[:, 0], "dp", ring))
        own = together(gathered)
        holds = [own]
        for step in range(1, groups):
            ring = [
                (i, target(i // members, step, groups) * members + i % members) for i in range(peers)
            ]
            holds.append(lax.ppermute(own, "dp", ring))
        feat = features_of(
            seed,
            lengths[None, :],
            mask.T,
            act.reshape(ckpts, examples * slots, rank),
            grad.reshape(ckpts, examples * slots, width),
            var[:, 0],
            cols,
        )
        pieces = list(scores_of(weight[None, :], feat, holds, parts))
        for step in range(1, parts):
            ring = [(i, (i + step) % parts) for i in range(parts)]
            pieces[step] = lax.ppermute(pieces[step], "layer", ring)
        vmem = pl.BlockSpec(memory_space=pltpu.VMEM)
        return pl.pallas_call(
            finish_kernel,
            out_shape=jax.ShapeDtypeStruct((examples // parts, peers * hold.shape[2]), F32),
            in_specs=[vmem] * parts,
            out_specs=vmem,
            compiler_params=pltpu.CompilerParams(vmem_limit_bytes=12 << 20),
            name="finish",
        )(*pieces)

    placed = (
        P(None, "layer", "dp", None, None),
        P(None, "layer", "dp", None, None),
        P(None, "layer", None, None),
        P(None, "layer", "dp", None),
        P("dp"),
        P("dp", None),
        P(),
        P(),
    )
    return jax.shard_map(
        local, mesh=mesh, in_specs=placed, out_specs=P(("dp", "layer"), None), check_vma=False
    )
```
